32 devices in a mesh: batch: 16 (over z, x, core), head: 2 (over y).
Axes of the slice: x: 2, y: 2, z: 4, core: 2. Of those that a mesh axis runs over, the one named last changes fastest.
Arguments:
- inputs: bfloat16 [32, 512, 768], P('batch', 'head'), may hold values from -6 to 6
- cotangent: bfloat16 [32, 512, 768], P('batch', 'head'), may hold values from -6 to 6
- seg_ids: int32 [32, 512], P('batch'), may hold values from 0 to 15, as said below
- pad_mask: int32 [32, 512], P('batch'), may hold values from 0 to 1, as said below
- attn_gain: bfloat16 [768], replicated, may hold values from 0.5 to 1.5
- attn_shift: bfloat16 [768], replicated, may hold values from -1 to 1
- w_query: bfloat16 [768, 768], P(None, 'head'), may hold values from -0.21875 to 0.21875
- w_key: bfloat16 [768, 768], P(None, 'head'), may hold values from -0.21875 to 0.21875
- w_value: bfloat16 [768, 768], P(None, 'head'), may hold values from -0.21875 to 0.21875
- b_query: bfloat16 [768], P('head'), may hold values from -1 to 1
- b_key: bfloat16 [768], P('head'), may hold values from -1 to 1
- b_value: bfloat16 [768], P('head'), may hold values from -1 to 1
- compress: bfloat16 [256, 512], P('head'), may hold values from -1.5 to 1.5
- w_out: bfloat16 [768, 768], P('head'), may hold values from -0.4375 to 0.4375
- b_out: bfloat16 [768], replicated, may hold values from -1 to 1
- ffn_gain: bfloat16 [768], replicated, may hold values from 0.5 to 1.5
- ffn_shift: bfloat16 [768], replicated, may hold values from -1 to 1
- w_up: bfloat16 [768, 3072], P(None, 'head'), may hold values from -0.21875 to 0.21875
- b_up: bfloat16 [3072], P('head'), may hold values from -1 to 1
- w_down: bfloat16 [3072, 768], P('head'), may hold values from -0.15625 to 0.15625
- b_down: bfloat16 [768], replicated, may hold values from -1 to 1
Outputs:
- output: bfloat16 [32, 512, 768], P('batch', 'head')
- input_grad: bfloat16 [32, 512, 768], P('batch', 'head')
- grad_attn_gain: float32 [768], replicated
- grad_attn_shift: float32 [768], replicated
- grad_w_query: float32 [768, 768], P(None, 'head')
- grad_w_key: float32 [768, 768], P(None, 'head')
- grad_w_value: float32 [768, 768], P(None, 'head')
- grad_b_query: float32 [768], P('head')
- grad_b_key: float32 [768], P('head')
- grad_b_value: float32 [768], P('head')
- grad_compress: float32 [256, 512], P('head')
- grad_w_out: float32 [768, 768], P('head')
- grad_b_out: float32 [768], replicated
- grad_ffn_gain: float32 [768], replicated
- grad_ffn_shift: float32 [768], replicated
- grad_w_up: float32 [768, 3072], P(None, 'head')
- grad_b_up: float32 [3072], P('head')
- grad_w_down: float32 [3072, 768], P('head')
- grad_b_down: float32 [768], replicated
The draws below stay inside these ranges and needn't reach their ends.
Inputs may be any that keep to these rules, and one draw needn't show every extreme that they name: `seg_ids`: in each row the ids start at 0 and never fall, and the row holds exactly 16 documents; ids change only at multiples of 2 tokens, and position 256 never starts a document. `pad_mask`: padding is a tail of each row, a multiple of 2 tokens long and at most 64 tokens.
All inputs are finite; a program needn't handle non-finite values.
Results may differ from the reference program's by a relative error of at most 0.018.
The reference program's roundings to bfloat16 on the way count: a program that leaves them out, or rounds other values in their place, can miss the bound.
Values may be sent and summed in bfloat16 or wider, within the bound.
A program may use at most 128 MiB of HBM per device.

```python
import math
import jax
import jax.numpy as jnp
from jax import lax

D = 768
H = 12
DH = 64
FF = 3072
KP = 256
SEQ = 512
ROWS = 32


def draw_seg_ids(key, part):
    doc_count = max(KP // 16, 2)
    unit_pos = jnp.arange(KP, dtype=jnp.int32)[None, :]
    noise = jax.random.randint(jax.random.fold_in(key, 11), (ROWS, KP), 0, 1 << 20)
    ranked = noise * KP + unit_pos
    excluded = (unit_pos == 0) | (unit_pos == KP // 2)
    ranked = jnp.where(excluded, 1 << 30, ranked)
    order = jnp.argsort(ranked, axis=1, stable=True)
    chosen = order[:, :doc_count - 1]
    flags = jnp.any(chosen[:, :, None] == unit_pos[:, None, :], axis=1).astype(jnp.int32)
    flags = jnp.where(unit_pos == 0, 1, flags)
    unit_ids = jnp.cumsum(flags, axis=1) - 1
    return jnp.repeat(unit_ids, SEQ // KP, axis=1).astype(jnp.int32)


def draw_pad_mask(key, part):
    tail_units = jax.random.randint(jax.random.fold_in(key, 23), (ROWS, 1), 0, KP // 8 + 1)
    unit_pos = jnp.arange(KP)[None, :]
    padded = (unit_pos >= KP - tail_units).astype(jnp.int32)
    return jnp.repeat(padded, SEQ // KP, axis=1).astype(jnp.int32)


def shard_levels(own_key, dims, cuts, low, top_value):
    def one(dim, parts):
        draws = jax.random.uniform(jax.random.fold_in(jax.random.fold_in(own_key, 6), dim), (parts,), jnp.float32, low / len(cuts), top_value / len(cuts))
        return jnp.repeat(jnp.exp(draws), dims[dim] // parts).reshape((-1,) + (1,) * (len(dims) - dim - 1))

    loudness = one(*cuts[0])
    for cut in cuts[1:]:
        loudness = loudness * one(*cut)
    return loudness


def centred(own_key, extent, deviation, limit, cuts=(), kind=jnp.bfloat16):
    factor_of = shard_levels(own_key, extent, cuts, -0.22, 0.18) if cuts else 1.0
    values = jax.random.normal(own_key, extent, jnp.float32) * deviation * factor_of
    return jnp.minimum(jnp.maximum(values, -limit), limit).astype(kind)


def setup_inputs(seed: int = 0) -> dict:
    key_of = jax.random.split(jax.random.key(seed), 22)
    inputs = centred(key_of[0], (ROWS, SEQ, D), 1.0, 6.0, ((0, 16), (1, 2)))
    cotangent = centred(key_of[1], (ROWS, SEQ, D), 1.0, 6.0, ((0, 16), (1, 2)))
    seg_ids = draw_seg_ids(jax.random.fold_in(key_of[21], 71), 0)
    pad_mask = draw_pad_mask(jax.random.fold_in(key_of[21], 71), 0)
    attn_gain = jnp.clip(1.0 + 0.1 * jax.random.normal(key_of[4], (D,), jnp.float32), 0.5, 1.5).astype(jnp.bfloat16)
    attn_shift = centred(key_of[5], (D,), 0.2, 1.0)
    w_query = centred(key_of[6], (D, D), D ** -0.5, 0.21875, ((1, 2),))
    w_key = centred(key_of[7], (D, D), D ** -0.5, 0.21875, ((1, 2),))
    w_value = centred(key_of[8], (D, D), D ** -0.5, 0.21875, ((1, 2),))
    b_query = centred(key_of[9], (D,), 0.2, 1.0, ((0, 2),))
    b_key = centred(key_of[10], (D,), 0.2, 1.0, ((0, 2),))
    b_value = centred(key_of[11], (D,), 0.2, 1.0, ((0, 2),))
    compress = centred(key_of[12], (KP, SEQ), 16 ** -0.5, 1.5, ((0, 2),))
    w_out = centred(key_of[13], (D, D), (D // 4) ** -0.5, 0.4375, ((0, 2),))
    b_out = centred(key_of[14], (D,), 0.2, 1.0)
    ffn_gain = jnp.clip(1.0 + 0.1 * jax.random.normal(key_of[15], (D,), jnp.float32), 0.5, 1.5).astype(jnp.bfloat16)
    ffn_shift = centred(key_of[16], (D,), 0.2, 1.0)
    w_up = centred(key_of[17], (D, FF), D ** -0.5, 0.21875, ((1, 2),))
    b_up = centred(key_of[18], (FF,), 0.2, 1.0, ((0, 2),))
    w_down = centred(key_of[19], (FF, D), (FF // 2) ** -0.5, 0.15625, ((0, 2),))
    b_down = centred(key_of[20], (D,), 0.2, 1.0)
    return dict(inputs=inputs, cotangent=cotangent, seg_ids=seg_ids, pad_mask=pad_mask, attn_gain=attn_gain, attn_shift=attn_shift, w_query=w_query, w_key=w_key, w_value=w_value, b_query=b_query, b_key=b_key, b_value=b_value, compress=compress, w_out=w_out, b_out=b_out, ffn_gain=ffn_gain, ffn_shift=ffn_shift, w_up=w_up, b_up=b_up, w_down=w_down, b_down=b_down)


@jax.custom_vjp
def low(v):
    return lax.optimization_barrier(v.astype(jnp.bfloat16)).astype(jnp.float32)

@jax.custom_vjp
def low_back(v):
    return v

def low_keep(v):
    return (low(v), None)

def low_pass(kept, grad):
    return (grad,)

def back_keep(v):
    return (v, None)

def back_low(kept, grad):
    return (low(grad),)
low.defvjp(low_keep, low_pass)
low_back.defvjp(back_keep, back_low)
NORM_EPS = 1e-05

def rows_normalize(values, gain_vector, offset_vector):
    mean_val = lax.optimization_barrier(jnp.mean(values, -1, keepdims=True))
    centered_rows = values - mean_val
    inverse_deviation = lax.rsqrt(lax.optimization_barrier(jnp.mean(centered_rows * centered_rows, -1, keepdims=True)) + NORM_EPS)
    return centered_rows * inverse_deviation * gain_vector + offset_vector

def forward(inputs, params, seg_ids, pad_mask):
    attn_gain, attn_shift, w_query, w_key, w_value, b_query, b_key, b_value, compress, w_out, b_out, ffn_gain, ffn_shift, w_up, b_up, w_down, b_down = params
    highest = lax.Precision.HIGHEST
    row_count = inputs.shape[0]
    normed_in = low(rows_normalize(inputs, attn_gain, attn_shift))
    query = low(low_back(jnp.einsum('rtd,de->rte', normed_in, w_query, precision=highest) + b_query))
    keys = low(low_back(jnp.einsum('rtd,de->rte', normed_in, w_key, precision=highest) + b_key))
    values = low(low_back(jnp.einsum('rtd,de->rte', normed_in, w_value, precision=highest) + b_value))
    slot_step = SEQ // KP
    slot_seg = seg_ids[:, ::slot_step]
    emask = (slot_seg[:, :, None] == seg_ids[:, None, :]) & (pad_mask[:, None, :] == 0)
    masked = jnp.where(emask, compress[None], 0.0)
    keys_c = low(low_back(jnp.einsum('rjt,rte->rje', masked, keys, precision=highest)))
    values_c = low(low_back(jnp.einsum('rjt,rte->rje', masked, values, precision=highest)))
    query4 = query.reshape(row_count, SEQ, H, DH)
    keys4 = keys_c.reshape(row_count, KP, H, DH)
    values4 = values_c.reshape(row_count, KP, H, DH)
    scores = low_back(jnp.einsum('rthe,rjhe->rhtj', query4, keys4, precision=highest) * DH ** (-0.5))
    slot_match = (seg_ids[:, :, None] == slot_seg[:, None, :])[:, None]
    scores = jnp.where(slot_match, scores, -1e+30)
    probs = jax.nn.softmax(scores, axis=-1)
    mixed = low(low_back(jnp.einsum('rhtj,rjhe->rthe', low(probs), values4, precision=highest)))
    mixed = mixed.reshape(row_count, SEQ, D)
    residual_stream = inputs + (low_back(jnp.einsum('rte,ed->rtd', mixed, w_out, precision=highest)) + b_out)
    normed_mid = low(rows_normalize(residual_stream, ffn_gain, ffn_shift))
    pre_act = low_back(jnp.einsum('rtd,df->rtf', normed_mid, w_up, precision=highest) + b_up)
    hidden = low(jax.nn.gelu(pre_act, approximate=False))
    return residual_stream + (jnp.einsum('rtf,fd->rtd', hidden, w_down, precision=highest) + b_down)

def reference(inputs, cotangent, seg_ids, pad_mask, attn_gain, attn_shift, w_query, w_key, w_value, b_query, b_key, b_value, compress, w_out, b_out, ffn_gain, ffn_shift, w_up, b_up, w_down, b_down):
    params = tuple((weight_arg.astype(jnp.float32) for weight_arg in (attn_gain, attn_shift, w_query, w_key, w_value, b_query, b_key, b_value, compress, w_out, b_out, ffn_gain, ffn_shift, w_up, b_up, w_down, b_down)))
    group_rows = math.gcd(ROWS, 8)
    blocks = ROWS // group_rows

    def split_rows(array_in):
        return array_in.reshape((blocks, group_rows) + array_in.shape[1:])

    def step_block(carry, item):
        in_block, cot_block, seg_block, pad_block = item

        def run_layer(in_val, *param_vals):
            return forward(in_val, param_vals, seg_block, pad_block)
        out_val, pull = jax.vjp(run_layer, in_block.astype(jnp.float32), *params)
        grads = pull(cot_block.astype(jnp.float32))
        summed = tuple((total_val + gradient_value for total_val, gradient_value in zip(carry, grads[1:])))
        return (summed, (out_val.astype(jnp.bfloat16), grads[0].astype(jnp.bfloat16)))
    init = tuple((jnp.zeros(param_val.shape, jnp.float32) for param_val in params))
    totals, (out_blocks, grad_blocks) = lax.scan(step_block, init, (split_rows(inputs), split_rows(cotangent), split_rows(seg_ids), split_rows(pad_mask)))
    return (out_blocks.reshape(ROWS, SEQ, D), grad_blocks.reshape(ROWS, SEQ, D), totals[0], totals[1], totals[2], totals[3], totals[4], totals[5], totals[6], totals[7], totals[8], totals[9], totals[10], totals[11], totals[12], totals[13], totals[14], totals[15], totals[16])
```

```python
import jax
import jax.numpy as jnp
from jax import lax
from jax.experimental import pallas as pl
from jax.experimental.pallas import tpu as pltpu
from jax.sharding import PartitionSpec as P

F32, BF16 = jnp.float32, jnp.bfloat16
T, D, KP = 512, 768, 256
NP_, NF = 6, 12
UNITS = 9
ROWS = 1536
SUB = 4
PART = ROWS // SUB
TOTAL = UNITS * SUB
EPS = 1e-5
SQRT_HALF = 0.7071067811865476
INV_SQRT_TWO_PI = 0.3989422804014327
MESH = pl.DeviceIdType.MESH
MIB = 1 << 20


def nn(a, b):
    return jnp.dot(a, b, preferred_element_type=F32)


def nt(a, b):
    return lax.dot_general(a, b, (((1,), (1,)), ((), ())), preferred_element_type=F32)


def norm_stats(v):
    mu = jnp.mean(v, -1, keepdims=True)
    c = v - mu
    rstd = lax.rsqrt(jnp.mean(c * c, -1, keepdims=True) + EPS)
    return c * rstd, rstd


def norm_back(g_out, xhat, rstd, gain):
    g = g_out * gain
    mg = jnp.mean(g, -1, keepdims=True)
    mp = jnp.mean(g * xhat, -1, keepdims=True)
    return rstd * (g - mg - xhat * mp)


def row_vec(ref):
    return ref[...].astype(F32).reshape(1, ref.shape[0])


def blocks(n, size, body):
    def step(i, carry):
        body(pl.ds(pl.multiple_of(i * size, size), size))
        return carry
    lax.fori_loop(0, n // size, step, 0)


class Refs:
    pass


HEAD = 0
GAPS = (2, 4, 3, 2, 2, 2, 3, 5, 5)


def gap(stage):
    return GAPS[min(stage, len(GAPS) - 1)]


def slots(stage):
    return 2 * gap(stage)


def orders(n):
    return {16: [(HEAD, 2, 4, 8)], 128: [(HEAD, 2, 4, 16, 8, 32, 64)]}[n]


def landing(rows, order):
    out, both = [], 2
    for axis in order:
        if axis == HEAD:
            both = 1
            out.append(rows)
        else:
            rows = rows if rows % 16 else rows // 2
            out.append(both * rows)
    return out


def attn_forward(r, p):
    lane = lax.broadcasted_iota(jnp.int32, (KP, 128), 1) < 64
    row = lax.broadcasted_iota(jnp.int32, (128, KP), 0) < 64
    zero = jnp.zeros((), BF16)
    g = p // 3
    bias = r.bias[g * 9 + p - g * 3]
    qkv = (nn(r.nin[...], r.wa[p, 0:D, :]) + bias).astype(BF16)
    r.qkv[p] = qkv
    kvc = nn(r.e[...], qkv[:, 128:]).astype(BF16)
    r.kvc[p] = kvc
    kc = kvc[:, :128] * jnp.asarray(0.125, BF16)
    kst = jnp.concatenate([jnp.where(lane, kc, zero), jnp.where(lane, zero, kc)], 0)
    r.s[...] = nt(kst, qkv[:, :128])
    for h in range(2):
        for t in range(4):
            rs, ts = pl.ds(h * KP, KP), pl.ds(t * 128, 128)
            s = r.s[rs, ts] + r.smask[:, ts]
            m = jnp.max(s, 0, keepdims=True)
            e = jnp.exp(s - m)
            inv = 1.0 / jnp.sum(e, 0, keepdims=True)
            r.p[p, rs, ts] = (e * inv).astype(BF16)
    vt = kvc[:, 128:].T
    lhs = jnp.concatenate([jnp.where(row, vt, zero), jnp.where(row, zero, vt)], 1)
    mt = nn(lhs, r.p[p]).astype(BF16)
    r.mixt[p] = mt
    r.mix[p] = mt.T


def w_out(r, p):
    return jnp.concatenate([r.wa[p, 768:896, :], r.wa[p, 896:1024, :]], 1)


def attn_backward(r, p, g, unit):
    lane = lax.broadcasted_iota(jnp.int32, (KP, 128), 1) < 64
    row = lax.broadcasted_iota(jnp.int32, (128, KP), 0) < 64
    zero = jnp.zeros((), BF16)
    dm = nt(r.drl[...], w_out(r, p)).astype(BF16)
    kvc = r.kvc[p]
    qkv = r.qkv[p]
    vc = kvc[:, 128:]
    vst = jnp.concatenate([jnp.where(lane, vc, zero), jnp.where(lane, zero, vc)], 0)
    r.s[...] = nt(vst, dm)
    for h in range(2):
        for t in range(4):
            rs, ts = pl.ds(h * KP, KP), pl.ds(t * 128, 128)
            pr = r.p[p, rs, ts].astype(F32)
            dp = r.s[rs, ts]
            c = jnp.sum(pr * dp, 0, keepdims=True)
            r.ds[rs, ts] = (pr * (dp - c)).astype(BF16)
    dvs = nn(r.p[p], dm)
    dks = nn(r.ds[...], qkv[:, :128]) * 0.125
    dkv = jnp.concatenate([jnp.where(lane, dks[:KP], dks[KP:]), jnp.where(lane, dvs[:KP], dvs[KP:])], 1).astype(BF16)
    kt = (kvc[:, :128] * jnp.asarray(0.125, BF16)).T
    lhs = jnp.concatenate([jnp.where(row, kt, zero), jnp.where(row, zero, kt)], 1)
    dq = nn(lhs, r.ds[...]).astype(BF16).T
    dkvt = nn(r.et[...], dkv).astype(BF16)
    r.dcomp[...] += nt(dkv, qkv[:, 128:])
    dqkv = jnp.concatenate([dq, dkvt], 1)
    gw = nn(r.nint[...], dqkv).astype(BF16)
    for j in range(3):
        for ch in range(2):
            r.grad[unit, ch, g, j * 384:(j + 1) * 384, :] = gw[ch * 384:(ch + 1) * 384, j * 128:(j + 1) * 128]
    r.gbqkv[p] = jnp.sum(dqkv.astype(F32), 0, keepdims=True)
    r.dmid[...] += nt(dqkv, r.wa[p, 0:D, :])
    gw = nn(r.mixt[p], r.drl[...]).astype(BF16)
    for j in range(6):
        lo = 1152 + (j % 3) * 128
        r.grad[unit, j // 3, g, lo:lo + 128, :] = gw[:, j * 128:(j + 1) * 128]


def ffn_chunk(r, k, g):
    c = g * 6 + k
    wup = r.wf[c, 0:D, :]
    wdn = jnp.concatenate([r.wf[c, 768 + 256 * j:1024 + 256 * j, :] for j in range(3)], 1)
    bup = r.bias[g * 9 + 3 + k][:, :256]
    for i in range(4):
        rs = pl.ds(i * 128, 128)
        pre = nn(r.nmid[rs, :], wup) + bup
        dh = nt(r.cot[rs, :], wdn)
        phi = 0.5 * (1.0 + lax.erf(pre * SQRT_HALF))
        pdf = jnp.exp(-0.5 * pre * pre) * INV_SQRT_TWO_PI
        r.ds[rs, 0:256] = (pre * phi).astype(BF16)
        r.ds[rs, 256:512] = (dh * (phi + pre * pdf)).astype(BF16)
        r.ffn[rs, :] += nn(r.ds[rs, 0:256], wdn)
        r.dmid[rs, :] += nt(r.ds[rs, 256:512], wup)
    gw = nn(r.ds[:, 0:256].T, r.cot[...]).astype(BF16)
    for j in range(6):
        lo = 768 + (j % 3) * 256
        r.grad[k, j // 3, g, lo:lo + 256, :] = gw[:, j * 128:(j + 1) * 128]
    gw = nn(r.nmidt[...], r.ds[:, 256:512]).astype(BF16)
    for ch in range(2):
        r.grad[k, ch, g, 0:768, :] = gw[:, ch * 128:(ch + 1) * 128]
    r.gbup[c] = jnp.sum(r.ds[:, 256:512].astype(F32), 0, keepdims=True)


def add_rows(dst, srcs, out=None):
    n = dst.shape[0]
    out = dst if out is None else out
    size = next(s for s in (256, 192, 128, 96, 64, 48, 32, 24, 16, 8) if n % s == 0)

    def body(rows):
        acc = dst[rows, :].astype(F32)
        for s in srcs:
            acc = acc + s[rows, :].astype(F32)
        out[rows, :] = acc.astype(BF16)
    blocks(n, size, body)


def part_of(u):
    if isinstance(u, int):
        return u // SUB, pl.ds(u % SUB * PART, PART)
    return lax.div(u, SUB), pl.ds(pl.multiple_of(lax.rem(u, SUB) * PART, PART), PART)


class Reduce:
    def __init__(self, r, n):
        self.r = r
        b, h = lax.axis_index("batch"), lax.axis_index("head")
        self.b, self.h, self.c = b, h, lax.rem(b, 2)
        self.core = (b + 1 - 2 * self.c, h)
        self.flip = (b, 1 - h)
        self.orders = orders(n)
        self.families = len(self.orders)

    def bit(self, stride):
        return lax.rem(lax.div(self.b, stride), 2)

    def across(self, stride):
        return (self.b + stride - 2 * stride * self.bit(stride), self.h)

    def copy(self, src, dst, stage, u, dev, j=0):
        slot = lax.rem(u, slots(stage))
        return lambda: pltpu.make_async_remote_copy(src_ref=src, dst_ref=dst, send_sem=self.r.rsend.at[stage, slot, j],
                                                    recv_sem=self.r.rrecv.at[stage, slot, j], device_id=dev, device_id_type=MESH)

    def exchanges(self, u, family, bufs):
        grad, rc, halves, fin = bufs
        one = rc.shape[0] == 1
        h, c, order = self.h, self.c, self.orders[family]
        slot = 0 if one else lax.rem(u, slots(0))
        none = lambda: None

        def core_add():
            for g in range(2):
                add_rows(grad.at[c, g], [rc.at[slot, g]])
        stages = [([self.copy(grad.at[1 - c], rc.at[slot], 0, u, self.core)], core_add)]
        base, part, both, gathers = 0, grad.shape[2], True, []
        for i, axis in enumerate(order):
            buf, last = halves[i], i == len(order) - 1
            dev = self.flip if axis == HEAD else self.across(axis)
            if axis == HEAD or part % 16:
                rows = send = pl.ds(base, part)
            else:
                part //= 2
                bit = self.bit(axis)
                send = pl.ds(pl.multiple_of(base + (1 - bit) * part, part), part)
                base = pl.multiple_of(base + bit * part, part)
                rows = pl.ds(base, part)
                gathers.append((axis, base, part))
            if axis == HEAD:
                both = False
                moves = [(1 - h, h, 0)]
            else:
                moves = [(0, 0, 0), (1, 1, part)] if both else [(h, h, 0)]
            lands = [buf.at[0 if one else lax.rem(u, slots(1 + i)), pl.ds(at, part)] for _, _, at in moves]
            cps = [self.copy(grad.at[c, g, send], land, 1 + i, u, dev, j) for j, ((g, _, _), land) in enumerate(zip(moves, lands))]

            def add(moves=moves, lands=lands, rows=rows, last=last):
                for (_, g, _), land in zip(moves, lands):
                    add_rows(grad.at[c, g, rows], [land], fin.at[c, rows] if last else None)
            stages.append((cps, add))
        for axis, lo, count in reversed(gathers):
            own = fin.at[c, pl.ds(lo, count)]
            stages.append(([self.copy(own, own, len(stages), u, self.across(axis))], none))
        stages.append(([self.copy(fin.at[c], fin.at[c], len(stages), u, self.core)], none))
        return stages

    def lags(self):
        count = len(self.exchanges(0, 0, self.bufs(0)))
        out = [0]
        for i in range(count):
            out.append(out[-1] + gap(i))
        return out

    def small(self):
        r = self.r
        return (r.cgrad, r.crc, r.chalves, r.cfin)

    def bufs(self, u):
        r = self.r
        at, rows = part_of(u)
        return (r.grad.at[at, :, :, rows], r.rc, r.halves, r.fin.at[at, :, rows])

    def step(self, u, i, family, bufs, done):
        st = self.exchanges(u, family, bufs)
        if i > len(st):
            return
        if i > 0:
            for cp in st[i - 1][0]:
                cp().wait()
            st[i - 1][1]()
        if i < len(st):
            for cp in st[i][0]:
                cp().start()
        else:
            done(u)

    def tick(self, i, lags, done, static):
        for s in reversed(range(len(lags))):
            u = i - lags[s]
            if static:
                if 0 <= u < TOTAL:
                    self.step(u, s, u % self.families, self.bufs(u), done)
                elif u == TOTAL:
                    self.step(u, s, 0, self.small(), lambda u: self.r.out_small())
                continue
            if s == 0:
                @pl.when((u >= 0) & (u < TOTAL))
                def _(s=s, u=u):
                    self.step(u, s, 0, self.bufs(u), done)
                continue
            for f in range(self.families):
                @pl.when((u >= 0) & (u < TOTAL) & (lax.rem(u, self.families) == f))
                def _(s=s, u=u, f=f):
                    self.step(u, s, f, self.bufs(u), done)


class Gather:
    def __init__(self, r, red):
        self.r = r
        self.h = red.h
        c, x, z = red.bit(1), red.bit(2), red.bit(4)
        self.q = (c * 4 + z * 2 + x, c * 4 + x * 2 + z)
        self.dev = [(red.flip, red.across(2), red.across(4), red.core), (red.flip, red.across(4), red.across(2), red.core)]

    def copy(self, u, stage, attn, odd):
        h = self.h
        g = h if stage == 0 else 1 - h
        unit = self.r.wa.at[g * 3 + u] if attn else self.r.wf.at[g * 6 + u - 3]
        piece = unit.shape[0] // 8
        count = 1 if stage == 0 else 1 << (stage - 1)
        lo = lax.div(self.q[odd], count) * count * piece
        view = unit.at[pl.ds(pl.multiple_of(lo, piece), count * piece)]
        return pltpu.make_async_remote_copy(src_ref=view, dst_ref=view, send_sem=self.r.gsend.at[u, stage], recv_sem=self.r.grecv.at[u, stage],
                                            device_id=self.dev[odd][stage], device_id_type=MESH)

    def start(self, u):
        self.copy(u, 0, u < 3, u % 2).start()

    def step(self, u, stage):
        self.copy(u, stage - 1, u < 3, u % 2).wait()
        if stage < 4:
            self.copy(u, stage, u < 3, u % 2).start()

    def ready(self, u, attn):
        for odd in range(2):
            @pl.when(lax.rem(u, 2) == odd)
            def _(odd=odd):
                self.copy(u, 3, attn, odd).wait()


def layer(n, names, refs):
    r = Refs()
    for name, ref in zip(names, refs):
        setattr(r, name, ref)
    steps = len(orders(n)[0])
    r.halves = [getattr(r, "half%d" % i) for i in range(steps)]
    r.chalves = [getattr(r, "chalf%d" % i) for i in range(steps)]
    red = Reduce(r, n)
    gat = Gather(r, red)
    b, h = red.b, red.h

    barrier = pltpu.get_barrier_semaphore()
    peers = [red.core, red.flip] + [red.across(axis) for axis in red.orders[0] if axis != HEAD]
    for dev in peers:
        pl.semaphore_signal(barrier, inc=1, device_id=dev, device_id_type=MESH)

    sem = iter(range(64))
    own = {}

    def load(key, src, dst):
        cp = pltpu.make_async_copy(src, dst, r.lsem.at[next(sem)])
        cp.start()
        own.setdefault(key, []).append(cp)

    def loaded(key):
        for cp in own[key]:
            cp.wait()

    hs = pl.ds(pl.multiple_of(h * 256, 256), 256)
    for u in range(3):
        unit, cols = r.wa.at[h * 3 + u], pl.ds(u * 128, 128)
        for j, w in enumerate((r.w_query, r.w_key, r.w_value)):
            load(u, w.at[:, cols], unit.at[0:768, j * 128:(j + 1) * 128])
        for j in range(2):
            load(u, r.w_out.at[cols, j * 384:(j + 1) * 384], unit.at[768 + 128 * j:896 + 128 * j])
    load("x", r.inputs.at[h], r.x.at[hs])
    cs = pl.ds(pl.multiple_of(h * 128, 128), 128)
    load("c", r.compress, r.comp.at[cs])
    for k in range(6):
        unit = r.wf.at[h * 6 + k]
        load(3 + k, r.w_up.at[:, k * 256:(k + 1) * 256], unit.at[0:768])
        for j in range(3):
            load(3 + k, r.w_down.at[k * 256:(k + 1) * 256, j * 256:(j + 1) * 256], unit.at[768 + 256 * j:1024 + 256 * j])
    load("t", r.cotangent.at[h], r.cot.at[hs])
    bqkv = [row_vec(v) for v in (r.b_query, r.b_key, r.b_value)]
    bup = row_vec(r.b_up)
    for u in range(3):
        r.bias[h * 9 + u] = jnp.concatenate([v[:, u * 128:(u + 1) * 128] for v in bqkv], 1)
    for k in range(6):
        r.bias[h * 9 + 3 + k, :, 0:256] = bup[:, k * 256:(k + 1) * 256]
        r.bias[h * 9 + 3 + k, :, 256:384] = jnp.zeros((1, 128), F32)

    pl.semaphore_wait(barrier, len(peers))

    def swap(i, src, dst):
        return pltpu.make_async_remote_copy(src_ref=src, dst_ref=dst, send_sem=r.ssend.at[i], recv_sem=r.srecv.at[i],
                                            device_id=red.flip, device_id_type=MESH)
    bs = r.bias.at[pl.ds(h * 9, 9)]
    swaps = [swap(0, r.inputs.at[1 - h], r.x.at[hs]), swap(1, r.compress, r.comp.at[cs]), swap(2, bs, bs), swap(3, r.cotangent.at[1 - h], r.cot.at[hs])]
    for u in range(3):
        loaded(u)
        gat.start(u)
    for i in range(3):
        swaps[i].start()
    for u in range(3, 9):
        loaded(u)
        gat.start(u)
        if u == 4:
            swaps[3].start()

    seg = r.seg_ids[pl.ds(h, 1), :]
    pad = r.pad_mask[pl.ds(h, 1), :]
    jj = lax.broadcasted_iota(jnp.int32, (KP, T), 0)
    tt = lax.broadcasted_iota(jnp.int32, (KP, T), 1)
    slot = jnp.sum(jnp.where(tt == 2 * jj, seg, 0), 1, keepdims=True)
    same = slot == seg
    r.smask[...] = jnp.where(same, 0.0, -1e30)
    r.keep[...] = jnp.where(same & (pad == 0), 1.0, 0.0).astype(BF16)
    gain_a, shift_a, b_out, gain_f, shift_f, b_down = (row_vec(v) for v in (r.attn_gain, r.attn_shift, r.b_out, r.ffn_gain, r.ffn_shift, r.b_down))
    for u, stage in ((0, 1), (1, 1), (0, 2), (2, 1), (1, 2), (0, 3), (2, 2)):
        gat.step(u, stage)

    loaded("x")
    swaps[0].wait()
    gat.step(1, 3)

    def ln1(rs):
        xh, _ = norm_stats(r.x[rs, :].astype(F32))
        r.nin[rs, :] = (xh * gain_a + shift_a).astype(BF16)
    blocks(T, 64, ln1)
    r.nint[...] = r.nin[...].T
    loaded("c")
    swaps[1].wait()
    swaps[2].wait()
    e = jnp.where(r.keep[...].astype(F32) > 0.5, r.comp[...].astype(F32), 0.0)
    r.e[...] = e.astype(BF16)
    r.et[...] = e.T.astype(BF16)

    def hook(i, table):
        for at, todo in sorted(table.items()):
            @pl.when(i == at)
            def _(todo=todo):
                for u, stage in todo:
                    gat.step(u, stage)
    fore = {0: [(2, 3)], 3: [(3, 1)], 4: [(4, 1)], 5: [(3, 2)]}

    def pair(i, carry):
        far = lax.div(i, 3)
        g = lax.rem(h + far, 2)
        pp = i - 3 * far

        @pl.when(far == 1)
        def _():
            gat.ready(pp, True)
        attn_forward(r, g * 3 + pp)
        hook(i, fore)
        return carry
    lax.fori_loop(0, 6, pair, 0)

    def proj(rs):
        o = nn(r.mix[0, rs, :], w_out(r, 0))
        for p in range(1, NP_):
            o = o + nn(r.mix[p, rs, :], w_out(r, p))
        res = r.x[rs, :].astype(F32) + (o + b_out)
        r.res[rs, :] = res
        xh, _ = norm_stats(res)
        r.nmid[rs, :] = (xh * gain_f + shift_f).astype(BF16)
        r.ffn[rs, :] = res + b_down
        r.dmid[rs, :] = jnp.zeros_like(res)
    blocks(T, 128, proj)
    r.nmidt[...] = r.nmid[...].T
    gat.step(4, 2)
    loaded("t")
    swaps[3].wait()

    def out_copy(u):
        at, rows = part_of(u)
        return pltpu.make_async_copy(r.fin.at[at, :, rows], r.out_grad.at[at, :, rows], r.osem.at[u])

    def done(u):
        out_copy(u).start()

    lags = red.lags()

    def ticks(group):
        for j in range(SUB // 2):
            red.tick(group * (SUB // 2) + j, lags, done, False)

    late = {1: [(3, 3)], 2: [(4, 3), (5, 1), (6, 1)], 3: [(5, 2), (7, 1)], 4: [(6, 2), (8, 1)], 5: [(7, 2), (5, 3)], 6: [(8, 2)], 7: [(6, 3)],
            8: [(7, 3)], 9: [(8, 3)]}

    def main(i, carry):
        far = (1 - lax.rem(i, 2)) * jnp.minimum(i, 1) + lax.div(i, 11)
        k = lax.div(i + 1 - 2 * far, 2)

        @pl.when(far == 1)
        def _():
            gat.ready(3 + k, False)
        ffn_chunk(r, k, lax.rem(h + far, 2))
        hook(i, late)

        @pl.when(i > 1)
        def _():
            ticks(i - 2)
        return carry
    lax.fori_loop(0, 12, main, 0)

    r.vec[0] = jnp.zeros((16, D), F32)

    def ln2b(rs):
        xh, rstd = norm_stats(r.res[rs, :])
        dm = r.dmid[rs, :]
        cot = r.cot[rs, :].astype(F32)
        d = cot + norm_back(dm, xh, rstd, gain_f)
        r.res[rs, :] = d
        r.drl[rs, :] = d.astype(BF16)
        r.nmid[rs, :] = r.ffn[rs, :].astype(BF16)
        for i, v in ((2, d), (3, dm * xh), (4, dm), (5, cot)):
            r.vec[0, i:i + 1, :] += jnp.sum(v, 0, keepdims=True)
        r.dmid[rs, :] = jnp.zeros_like(d)
    blocks(T, 64, ln2b)
    ticks(10)
    r.dcomp[...] = jnp.zeros_like(r.dcomp)

    def back(i, carry):
        pp = lax.div(i, 2)
        g = lax.rem(h + i, 2)
        attn_backward(r, g * 3 + pp, g, 6 + pp)
        ticks(11 + i)
        return carry
    lax.fori_loop(0, 6, back, 0)
    gc = jnp.where(r.keep[...].astype(F32) > 0.5, r.dcomp[...], 0.0).astype(BF16)
    for g in range(2):
        for j in range(4):
            lo = (j % 2) * 128
            r.cgrad[j // 2, g, lo:lo + 128, :] = gc[g * 128:(g + 1) * 128, j * 128:(j + 1) * 128]

    def ln1b(rs):
        xh, rstd = norm_stats(r.x[rs, :].astype(F32))
        dn = r.dmid[rs, :]
        r.nin[rs, :] = (r.res[rs, :] + norm_back(dn, xh, rstd, gain_a)).astype(BF16)
        r.vec[0, 0:1, :] += jnp.sum(dn * xh, 0, keepdims=True)
        r.vec[0, 1:2, :] += jnp.sum(dn, 0, keepdims=True)
    blocks(T, 64, ln1b)
    for g in range(2):
        for i in range(2):
            at = 6 + g * 2 + i
            r.vec[0, at:at + 1, :] = jnp.concatenate([r.gbup[g * 6 + 3 * i + j] for j in range(3)], 1)
    for j in range(3):
        r.vec[0, 10 + j:11 + j, :] = jnp.concatenate([r.gbqkv[p][:, j * 128:(j + 1) * 128] for p in range(NP_)], 1)

    bits = [red.flip]
    s = 1
    while s < n:
        v = lax.rem(lax.div(b, s), 2)
        bits.append((b + s - 2 * s * v, h))
        s *= 2

    def vec_copy(i):
        return pltpu.make_async_remote_copy(src_ref=r.vec.at[i], dst_ref=r.vrecv.at[i], send_sem=r.vsend.at[i], recv_sem=r.vrsem.at[i],
                                            device_id=bits[i], device_id_type=MESH)

    def vec_step(i):
        if i > 0:
            vec_copy(i - 1).wait()
            r.vec[i] = r.vec[i - 1] + r.vrecv[i - 1]
        if i < len(bits):
            vec_copy(i).start()
    r.out_small = lambda: pltpu.make_async_copy(r.cfin, r.out_comp, r.osem.at[TOTAL]).start()

    hs_far = pl.ds(pl.multiple_of((1 - h) * 256, 256), 256)
    backs, locs = [], []
    for i, (src, dst) in enumerate(((r.nmid, r.out_y), (r.nin, r.out_ig))):
        backs.append(swap(4 + i, src.at[hs_far], dst.at[h]))
        cp = pltpu.make_async_copy(src.at[hs], dst.at[h], r.lsem.at[next(sem)])
        cp.start()
        locs.append(cp)
    vec_step(0)
    first = 17 * (SUB // 2)
    for i in range(first, TOTAL + lags[-1] + 1):
        red.tick(i, lags, done, True)
        if 1 <= i - first <= len(bits):
            vec_step(i - first)
        if i == TOTAL - 1 + lags[2]:
            for cp in backs:
                cp.start()
    cp = pltpu.make_async_copy(r.vec.at[len(bits)], r.out_vec, r.lsem.at[next(sem)])
    cp.start()
    locs.append(cp)
    for cp in backs + locs:
        cp.wait()
    for u in range(TOTAL):
        out_copy(u).wait()
    pltpu.make_async_copy(r.cfin, r.out_comp, r.osem.at[TOTAL]).wait()


ARGS = ["inputs", "cotangent", "seg_ids", "pad_mask", "attn_gain", "attn_shift", "w_query", "w_key", "w_value", "b_query", "b_key", "b_value",
        "compress", "w_out", "b_out", "ffn_gain", "ffn_shift", "w_up", "b_up", "w_down", "b_down"]
IN_HBM = ["inputs", "cotangent", "w_query", "w_key", "w_value", "compress", "w_out", "w_up", "w_down"]


def run_layer(n, args):
    bits = n.bit_length()
    out = dict(out_y=((2, 256, D), BF16), out_ig=((2, 256, D), BF16), out_grad=((UNITS, 2, ROWS, 128), BF16), out_comp=((2, 256, 128), BF16), out_vec=((16, D), F32))
    scr = dict(x=((T, D), BF16), cot=((T, D), BF16), comp=((KP, T), BF16), bias=((18, 1, 384), F32), wa=((NP_, 1024, 384), BF16), wf=((NF, ROWS, 256), BF16),
               e=((KP, T), BF16), et=((T, KP), BF16), smask=((KP, T), F32), keep=((KP, T), BF16), nin=((T, D), BF16), nint=((D, T), BF16),
               qkv=((NP_, T, 384), BF16), kvc=((NP_, KP, 256), BF16), s=((512, T), F32), p=((NP_, 512, T), BF16), ds=((512, T), BF16),
               mixt=((NP_, 128, T), BF16), mix=((NP_, T, 128), BF16), res=((T, D), F32), nmid=((T, D), BF16), nmidt=((D, T), BF16),
               ffn=((T, D), F32), dmid=((T, D), F32), drl=((T, D), BF16), dcomp=((KP, T), F32),
               vec=((bits + 1, 16, D), F32), vrecv=((bits, 16, D), F32),
               gbup=((NF, 1, 256), F32), gbqkv=((NP_, 1, 384), F32), grad=((UNITS, 2, 2, ROWS, 128), BF16), cgrad=((2, 2, 256, 128), BF16), fin=((UNITS, 2, ROWS, 128), BF16), cfin=((2, 256, 128), BF16))
    steps = len(orders(n)[0])
    for pre, rows in (("", PART), ("c", 256)):
        scr[pre + "rc"] = ((slots(0) if pre == "" else 1, 2, rows, 128), BF16)
        for i in range(steps):
            scr["%shalf%d" % (pre, i)] = ((slots(1 + i) if pre == "" else 1, max(landing(rows, order)[i] for order in orders(n)), 128), BF16)
    stages = 2 * steps + 1
    width = max(1 if order[0] == HEAD else 2 for order in orders(n))
    sems = dict(rsend=(stages, 2 * max(GAPS), width), rrecv=(stages, 2 * max(GAPS), width), gsend=(9, 4), grecv=(9, 4), ssend=(6,), srecv=(6,), vsend=(bits,), vrsem=(bits,),
                lsem=(48,), osem=(TOTAL + 1,))
    names = ARGS + list(out) + list(scr) + list(sems)
    hbm, vmem = pl.BlockSpec(memory_space=pl.ANY), pl.BlockSpec(memory_space=pltpu.VMEM)
    return pl.pallas_call(
        lambda *refs: layer(n, names, refs),
        out_shape=[jax.ShapeDtypeStruct(*v) for v in out.values()],
        in_specs=[hbm if a in IN_HBM else vmem for a in ARGS], out_specs=[hbm] * len(out),
        scratch_shapes=[pltpu.VMEM(*v) for v in scr.values()] + [pltpu.SemaphoreType.DMA(v) for v in sems.values()],
        compiler_params=pltpu.CompilerParams(collective_id=0, has_side_effects=True, vmem_limit_bytes=63 * MIB), name="layer")(*args)


def finish(refs):
    (y_in, ig_in, g_in, c_in, v_in, y, ig, gain_a, shift_a, wq, wk, wv, bq, bk, bv, comp, wo, bo, gain_f, shift_f, wu, bu, wd, bd,
     gbuf, cbuf, ybuf, igbuf, fa, fo, fu, fd, fc, isem, osem) = refs
    h = lax.axis_index("head")
    outs = iter(range(64))
    pend = []

    def put(src, dst):
        cp = pltpu.make_async_copy(src, dst, osem.at[next(outs)])
        cp.start()
        pend.append(cp)
    ins = [pltpu.make_async_copy(g_in.at[u], gbuf.at[u], isem.at[u]) for u in range(UNITS)]
    for i, (src, dst) in enumerate(((c_in, cbuf), (y_in, ybuf), (ig_in, igbuf))):
        ins.append(pltpu.make_async_copy(src, dst, isem.at[UNITS + i]))
    for cp in ins:
        cp.start()
    for i, o in enumerate((gain_a, shift_a, bo, gain_f, shift_f, bd)):
        o[...] = v_in[i, :]
    for i, o in enumerate((bq, bk, bv)):
        v = v_in[10 + i:11 + i, :]
        o[...] = jnp.where(h == 0, v[:, :384], v[:, 384:]).reshape(384)
    v = jnp.where(h == 0, v_in[6:8, :], v_in[8:10, :])
    bu[...] = jnp.concatenate([v[0:1], v[1:2]], 1).reshape(1536)
    for k in range(6):
        ins[k].wait()
        for ch in range(2):
            fu[k, :, ch * 128:(ch + 1) * 128] = gbuf[k, ch, 0:768, :].astype(F32)
            for j in range(3):
                at = (ch * 3 + j) * 128
                fd[k, :, at:at + 128] = gbuf[k, ch, 768 + j * 256:1024 + j * 256, :].astype(F32)
        put(fu.at[k], wu.at[:, k * 256:(k + 1) * 256])
        put(fd.at[k], wd.at[k * 256:(k + 1) * 256])
    for p in range(3):
        u = 6 + p
        ins[u].wait()
        for ch in range(2):
            for j in range(3):
                fa[j, ch * 384:(ch + 1) * 384, p * 128:(p + 1) * 128] = gbuf[u, ch, j * 384:(j + 1) * 384, :].astype(F32)
                at = (ch * 3 + j) * 128
                fo[p, :, at:at + 128] = gbuf[u, ch, 1152 + j * 128:1280 + j * 128, :].astype(F32)
        put(fo.at[p], wo.at[p * 128:(p + 1) * 128])
    for j, o in enumerate((wq, wk, wv)):
        put(fa.at[j], o)
    for cp in ins[UNITS:]:
        cp.wait()
    put(ybuf, y)
    put(igbuf, ig)
    for j in range(4):
        fc[:, j * 128:(j + 1) * 128] = cbuf[j // 2, (j % 2) * 128:(j % 2) * 128 + 128, :].astype(F32)
    put(fc, comp)
    for cp in pend:
        cp.wait()


def run_finish(parts):
    hbm, vmem = pl.BlockSpec(memory_space=pl.ANY), pl.BlockSpec(memory_space=pltpu.VMEM)
    f = lambda *s: jax.ShapeDtypeStruct(s, F32)
    row = jax.ShapeDtypeStruct((2, 256, D), BF16)
    outs = [(row, hbm), (row, hbm), (f(D), vmem), (f(D), vmem), (f(D, 384), hbm), (f(D, 384), hbm), (f(D, 384), hbm), (f(384), vmem), (f(384), vmem), (f(384), vmem),
            (f(128, T), hbm), (f(384, D), hbm), (f(D), vmem), (f(D), vmem), (f(D), vmem), (f(D, 1536), hbm), (f(1536), vmem), (f(1536, D), hbm), (f(D), vmem)]
    scr = [((UNITS, 2, ROWS, 128), BF16), ((2, 256, 128), BF16), ((2, 256, D), BF16), ((2, 256, D), BF16), ((3, D, 384), F32), ((3, 128, D), F32), ((6, D, 256), F32), ((6, 256, D), F32), ((128, T), F32)]
    return pl.pallas_call(
        lambda *refs: finish(refs), out_shape=[o for o, _ in outs], in_specs=[hbm] * 4 + [vmem], out_specs=[s for _, s in outs],
        scratch_shapes=[pltpu.VMEM(*v) for v in scr] + [pltpu.SemaphoreType.DMA((UNITS + 3,)), pltpu.SemaphoreType.DMA((64,))],
        compiler_params=pltpu.CompilerParams(vmem_limit_bytes=62 * MIB), name="finish")(*parts)


def solution(mesh):
    n = mesh.shape["batch"]

    def on_device(*args):
        return tuple(run_finish(run_layer(n, args)))

    tok, rep, col, vec, row = P("batch", "head", None), P(), P(None, "head"), P("head"), P("head", None)
    ids = P("batch", None)
    return jax.shard_map(
        on_device, mesh=mesh,
        in_specs=(tok, tok, ids, ids, rep, rep, col, col, col, vec, vec, vec, row, row, rep, rep, rep, col, vec, row, rep),
        out_specs=(tok, tok, rep, rep, col, col, col, vec, vec, vec, row, row, rep, rep, rep, col, vec, row, rep),
        check_vma=False)
```

```python
import jax
import jax.numpy as jnp
from jax import lax
from jax.experimental import pallas as pl
from jax.experimental.pallas import tpu as pltpu
from jax.sharding import PartitionSpec as P

F32, BF16 = jnp.float32, jnp.bfloat16
T, D, KP = 512, 768, 256
NP_, NF = 6, 12
UNITS = 9
ROWS = 1536
SUB = 4
PART = ROWS // SUB
TOTAL = UNITS * SUB
EPS = 1e-5
SQRT_HALF = 0.7071067811865476
INV_SQRT_TWO_PI = 0.3989422804014327
MESH = pl.DeviceIdType.MESH
MIB = 1 << 20


def nn(a, b):
    return jnp.dot(a, b, preferred_element_type=F32)


def nt(a, b):
    return lax.dot_general(a, b, (((1,), (1,)), ((), ())), preferred_element_type=F32)


def norm_stats(v):
    mu = jnp.mean(v, -1, keepdims=True)
    c = v - mu
    rstd = lax.rsqrt(jnp.mean(c * c, -1, keepdims=True) + EPS)
    return c * rstd, rstd


def norm_back(g_out, xhat, rstd, gain):
    g = g_out * gain
    mg = jnp.mean(g, -1, keepdims=True)
    mp = jnp.mean(g * xhat, -1, keepdims=True)
    return rstd * (g - mg - xhat * mp)


def row_vec(ref):
    return ref[...].astype(F32).reshape(1, ref.shape[0])


def blocks(n, size, body):
    def step(i, carry):
        body(pl.ds(pl.multiple_of(i * size, size), size))
        return carry
    lax.fori_loop(0, n // size, step, 0)


class Refs:
    pass


HEAD = 0
GAPS = (2, 4, 3, 2, 2, 2, 3, 5, 5)


def gap(stage):
    return GAPS[min(stage, len(GAPS) - 1)]


def slots(stage):
    return 2 * gap(stage)


def orders(n):
    return {16: [(HEAD, 2, 4, 8)], 128: [(HEAD, 2, 4, 16, 8, 32, 64)]}[n]


def landing(rows, order):
    out, both = [], 2
    for axis in order:
        if axis == HEAD:
            both = 1
            out.append(rows)
        else:
            rows = rows if rows % 16 else rows // 2
            out.append(both * rows)
    return out


def attn_forward(r, p):
    lane = lax.broadcasted_iota(jnp.int32, (KP, 128), 1) < 64
    row = lax.broadcasted_iota(jnp.int32, (128, KP), 0) < 64
    zero = jnp.zeros((), BF16)
    g = p // 3
    bias = r.bias[g * 9 + p - g * 3]
    qkv = (nn(r.nin[...], r.wa[p, 0:D, :]) + bias).astype(BF16)
    r.qkv[p] = qkv
    kvc = nn(r.e[...], qkv[:, 128:]).astype(BF16)
    r.kvc[p] = kvc
    kc = kvc[:, :128] * jnp.asarray(0.125, BF16)
    kst = jnp.concatenate([jnp.where(lane, kc, zero), jnp.where(lane, zero, kc)], 0)
    r.s[...] = nt(kst, qkv[:, :128])
    for h in range(2):
        for t in range(4):
            rs, ts = pl.ds(h * KP, KP), pl.ds(t * 128, 128)
            s = r.s[rs, ts] + r.smask[:, ts]
            m = jnp.max(s, 0, keepdims=True)
            e = jnp.exp(s - m)
            inv = 1.0 / jnp.sum(e, 0, keepdims=True)
            r.p[p, rs, ts] = (e * inv).astype(BF16)
    vt = kvc[:, 128:].T
    lhs = jnp.concatenate([jnp.where(row, vt, zero), jnp.where(row, zero, vt)], 1)
    mt = nn(lhs, r.p[p]).astype(BF16)
    r.mixt[p] = mt
    r.mix[p] = mt.T


def w_out(r, p):
    return jnp.concatenate([r.wa[p, 768:896, :], r.wa[p, 896:1024, :]], 1)


def attn_backward(r, p, g, unit):
    lane = lax.broadcasted_iota(jnp.int32, (KP, 128), 1) < 64
    row = lax.broadcasted_iota(jnp.int32, (128, KP), 0) < 64
    zero = jnp.zeros((), BF16)
    dm = nt(r.drl[...], w_out(r, p)).astype(BF16)
    kvc = r.kvc[p]
    qkv = r.qkv[p]
    vc = kvc[:, 128:]
    vst = jnp.concatenate([jnp.where(lane, vc, zero), jnp.where(lane, zero, vc)], 0)
    r.s[...] = nt(vst, dm)
    for h in range(2):
        for t in range(4):
            rs, ts = pl.ds(h * KP, KP), pl.ds(t * 128, 128)
            pr = r.p[p, rs, ts].astype(F32)
            dp = r.s[rs, ts]
            c = jnp.sum(pr * dp, 0, keepdims=True)
            r.ds[rs, ts] = (pr * (dp - c)).astype(BF16)
    dvs = nn(r.p[p], dm)
    dks = nn(r.ds[...], qkv[:, :128]) * 0.125
    dkv = jnp.concatenate([jnp.where(lane, dks[:KP], dks[KP:]), jnp.where(lane, dvs[:KP], dvs[KP:])], 1).astype(BF16)
    kt = (kvc[:, :128] * jnp.asarray(0.125, BF16)).T
    lhs = jnp.concatenate([jnp.where(row, kt, zero), jnp.where(row, zero, kt)], 1)
    dq = nn(lhs, r.ds[...]).astype(BF16).T
    dkvt = nn(r.et[...], dkv).astype(BF16)
    r.dcomp[...] += nt(dkv, qkv[:, 128:])
    dqkv = jnp.concatenate([dq, dkvt], 1)
    gw = nn(r.nint[...], dqkv).astype(BF16)
    for j in range(3):
        for ch in range(2):
            r.grad[unit, ch, g, j * 384:(j + 1) * 384, :] = gw[ch * 384:(ch + 1) * 384, j * 128:(j + 1) * 128]
    r.gbqkv[p] = jnp.sum(dqkv.astype(F32), 0, keepdims=True)
    r.dmid[...] += nt(dqkv, r.wa[p, 0:D, :])
    gw = nn(r.mixt[p], r.drl[...]).astype(BF16)
    for j in range(6):
        lo = 1152 + (j % 3) * 128
        r.grad[unit, j // 3, g, lo:lo + 128, :] = gw[:, j * 128:(j + 1) * 128]


def ffn_chunk(r, k, g):
    c = g * 6 + k
    wup = r.wf[c, 0:D, :]
    wdn = jnp.concatenate([r.wf[c, 768 + 256 * j:1024 + 256 * j, :] for j in range(3)], 1)
    bup = r.bias[g * 9 + 3 + k][:, :256]
    for i in range(4):
        rs = pl.ds(i * 128, 128)
        pre = nn(r.nmid[rs, :], wup) + bup
        dh = nt(r.cot[rs, :], wdn)
        phi = 0.5 * (1.0 + lax.erf(pre * SQRT_HALF))
        pdf = jnp.exp(-0.5 * pre * pre) * INV_SQRT_TWO_PI
        r.ds[rs, 0:256] = (pre * phi).astype(BF16)
        r.ds[rs, 256:512] = (dh * (phi + pre * pdf)).astype(BF16)
        r.ffn[rs, :] += nn(r.ds[rs, 0:256], wdn)
        r.dmid[rs, :] += nt(r.ds[rs, 256:512], wup)
    gw = nn(r.ds[:, 0:256].T, r.cot[...]).astype(BF16)
    for j in range(6):
        lo = 768 + (j % 3) * 256
        r.grad[k, j // 3, g, lo:lo + 256, :] = gw[:, j * 128:(j + 1) * 128]
    gw = nn(r.nmidt[...], r.ds[:, 256:512]).astype(BF16)
    for ch in range(2):
        r.grad[k, ch, g, 0:768, :] = gw[:, ch * 128:(ch + 1) * 128]
    r.gbup[c] = jnp.sum(r.ds[:, 256:512].astype(F32), 0, keepdims=True)


def add_rows(dst, src, out=None):
    out = dst if out is None else out
    n = dst.shape[0]
    for lo in range(0, n, 384):
        rows = pl.ds(lo, min(384, n - lo))
        out[rows, :] = dst[rows, :] + src[rows, :]


def part_of(u):
    if isinstance(u, int):
        return u // SUB, pl.ds(u % SUB * PART, PART)
    return lax.div(u, SUB), pl.ds(pl.multiple_of(lax.rem(u, SUB) * PART, PART), PART)


class Reduce:
    def __init__(self, r, n):
        self.r = r
        b, h = lax.axis_index("batch"), lax.axis_index("head")
        self.b, self.h, self.c = b, h, lax.rem(b, 2)
        self.core = (b + 1 - 2 * self.c, h)
        self.flip = (b, 1 - h)
        self.orders = orders(n)
        self.families = len(self.orders)

    def bit(self, stride):
        return lax.rem(lax.div(self.b, stride), 2)

    def across(self, stride):
        return (self.b + stride - 2 * stride * self.bit(stride), self.h)

    def copy(self, src, dst, stage, u, dev, j=0):
        slot = lax.rem(u, slots(stage))
        return lambda: pltpu.make_async_remote_copy(src_ref=src, dst_ref=dst, send_sem=self.r.rsend.at[stage, slot, j],
                                                    recv_sem=self.r.rrecv.at[stage, slot, j], device_id=dev, device_id_type=MESH)

    def exchanges(self, u, family, bufs):
        grad, rc, halves, fin = bufs
        one = rc.shape[0] == 1
        h, c, order = self.h, self.c, self.orders[family]
        slot = 0 if one else lax.rem(u, slots(0))
        none = lambda: None

        def core_add():
            for g in range(2):
                add_rows(grad.at[c, g], rc.at[slot, g])
        stages = [([self.copy(grad.at[1 - c], rc.at[slot], 0, u, self.core)], core_add)]
        base, part, both, gathers = 0, grad.shape[2], True, []
        for i, axis in enumerate(order):
            buf, last = halves[i], i == len(order) - 1
            dev = self.flip if axis == HEAD else self.across(axis)
            if axis == HEAD or part % 16:
                rows = send = pl.ds(base, part)
            else:
                part //= 2
                bit = self.bit(axis)
                send = pl.ds(pl.multiple_of(base + (1 - bit) * part, part), part)
                base = pl.multiple_of(base + bit * part, part)
                rows = pl.ds(base, part)
                gathers.append((axis, base, part))
            if axis == HEAD:
                both = False
                moves = [(1 - h, h, 0)]
            else:
                moves = [(0, 0, 0), (1, 1, part)] if both else [(h, h, 0)]
            lands = [buf.at[0 if one else lax.rem(u, slots(1 + i)), pl.ds(at, part)] for _, _, at in moves]
            cps = [self.copy(grad.at[c, g, send], land, 1 + i, u, dev, j) for j, ((g, _, _), land) in enumerate(zip(moves, lands))]

            def add(moves=moves, lands=lands, rows=rows, last=last):
                for (_, g, _), land in zip(moves, lands):
                    add_rows(grad.at[c, g, rows], land, fin.at[c, rows] if last else None)
            stages.append((cps, add))
        for axis, lo, count in reversed(gathers):
            own = fin.at[c, pl.ds(lo, count)]
            stages.append(([self.copy(own, own, len(stages), u, self.across(axis))], none))
        stages.append(([self.copy(fin.at[c], fin.at[c], len(stages), u, self.core)], none))
        return stages

    def lags(self):
        count = len(self.exchanges(0, 0, self.bufs(0)))
        out = [0]
        for i in range(count):
            out.append(out[-1] + gap(i))
        return out

    def small(self):
        r = self.r
        return (r.cgrad, r.crc, r.chalves, r.out_comp)

    def bufs(self, u):
        r = self.r
        at, rows = part_of(u)
        return (r.grad.at[at, :, :, rows], r.rc, r.halves, r.out_grad.at[at, :, rows])

    def step(self, u, i, family, bufs):
        st = self.exchanges(u, family, bufs)
        if i > len(st):
            return
        if i > 0:
            for cp in st[i - 1][0]:
                cp().wait()
            st[i - 1][1]()
        if i < len(st):
            for cp in st[i][0]:
                cp().start()

    def tick(self, i, lags, static):
        for s in reversed(range(len(lags))):
            u = i - lags[s]
            if static:
                if 0 <= u < TOTAL:
                    self.step(u, s, u % self.families, self.bufs(u))
                elif u == TOTAL:
                    self.step(u, s, 0, self.small())
                continue
            if s == 0:
                @pl.when((u >= 0) & (u < TOTAL))
                def _(s=s, u=u):
                    self.step(u, s, 0, self.bufs(u))
                continue
            for f in range(self.families):
                @pl.when((u >= 0) & (u < TOTAL) & (lax.rem(u, self.families) == f))
                def _(s=s, u=u, f=f):
                    self.step(u, s, f, self.bufs(u))


class Gather:
    def __init__(self, r, red):
        self.r = r
        self.h = red.h
        c, x, z = red.bit(1), red.bit(2), red.bit(4)
        self.q = (c * 4 + z * 2 + x, c * 4 + x * 2 + z)
        self.dev = [(red.flip, red.across(2), red.across(4), red.core), (red.flip, red.across(4), red.across(2), red.core)]

    def copy(self, u, stage, attn, odd):
        h = self.h
        g = h if stage == 0 else 1 - h
        unit = self.r.wa.at[g * 3 + u] if attn else self.r.wf.at[g * 6 + u - 3]
        piece = unit.shape[0] // 8
        count = 1 if stage == 0 else 1 << (stage - 1)
        lo = lax.div(self.q[odd], count) * count * piece
        view = unit.at[pl.ds(pl.multiple_of(lo, piece), count * piece)]
        return pltpu.make_async_remote_copy(src_ref=view, dst_ref=view, send_sem=self.r.gsend.at[u, stage], recv_sem=self.r.grecv.at[u, stage],
                                            device_id=self.dev[odd][stage], device_id_type=MESH)

    def start(self, u):
        self.copy(u, 0, u < 3, u % 2).start()

    def step(self, u, stage):
        self.copy(u, stage - 1, u < 3, u % 2).wait()
        if stage < 4:
            self.copy(u, stage, u < 3, u % 2).start()

    def ready(self, u, attn):
        for odd in range(2):
            @pl.when(lax.rem(u, 2) == odd)
            def _(odd=odd):
                self.copy(u, 3, attn, odd).wait()


def layer(n, names, refs):
    r = Refs()
    for name, ref in zip(names, refs):
        setattr(r, name, ref)
    steps = len(orders(n)[0])
    r.halves = [getattr(r, "half%d" % i) for i in range(steps)]
    r.chalves = [getattr(r, "chalf%d" % i) for i in range(steps)]
    red = Reduce(r, n)
    gat = Gather(r, red)
    b, h = red.b, red.h

    barrier = pltpu.get_barrier_semaphore()
    peers = [red.core, red.flip] + [red.across(axis) for axis in red.orders[0] if axis != HEAD]
    for dev in peers:
        pl.semaphore_signal(barrier, inc=1, device_id=dev, device_id_type=MESH)

    sem = iter(range(64))
    own = {}

    def load(key, src, dst):
        cp = pltpu.make_async_copy(src, dst, r.lsem.at[next(sem)])
        cp.start()
        own.setdefault(key, []).append(cp)

    def loaded(key):
        for cp in own[key]:
            cp.wait()

    hs = pl.ds(pl.multiple_of(h * 256, 256), 256)
    for u in range(3):
        unit, cols = r.wa.at[h * 3 + u], pl.ds(u * 128, 128)
        for j, w in enumerate((r.w_query, r.w_key, r.w_value)):
            load(u, w.at[:, cols], unit.at[0:768, j * 128:(j + 1) * 128])
        for j in range(2):
            load(u, r.w_out.at[cols, j * 384:(j + 1) * 384], unit.at[768 + 128 * j:896 + 128 * j])
    load("x", r.inputs.at[h], r.x.at[hs])
    cs = pl.ds(pl.multiple_of(h * 128, 128), 128)
    load("c", r.compress, r.comp.at[cs])
    for k in range(6):
        unit = r.wf.at[h * 6 + k]
        load(3 + k, r.w_up.at[:, k * 256:(k + 1) * 256], unit.at[0:768])
        for j in range(3):
            load(3 + k, r.w_down.at[k * 256:(k + 1) * 256, j * 256:(j + 1) * 256], unit.at[768 + 256 * j:1024 + 256 * j])
    load("t", r.cotangent.at[h], r.cot.at[hs])
    bqkv = [row_vec(v) for v in (r.b_query, r.b_key, r.b_value)]
    bup = row_vec(r.b_up)
    for u in range(3):
        r.bias[h * 9 + u] = jnp.concatenate([v[:, u * 128:(u + 1) * 128] for v in bqkv], 1)
    for k in range(6):
        r.bias[h * 9 + 3 + k, :, 0:256] = bup[:, k * 256:(k + 1) * 256]
        r.bias[h * 9 + 3 + k, :, 256:384] = jnp.zeros((1, 128), F32)

    pl.semaphore_wait(barrier, len(peers))

    def swap(i, src, dst):
        return pltpu.make_async_remote_copy(src_ref=src, dst_ref=dst, send_sem=r.ssend.at[i], recv_sem=r.srecv.at[i],
                                            device_id=red.flip, device_id_type=MESH)
    bs = r.bias.at[pl.ds(h * 9, 9)]
    swaps = [swap(0, r.inputs.at[1 - h], r.x.at[hs]), swap(1, r.compress, r.comp.at[cs]), swap(2, bs, bs), swap(3, r.cotangent.at[1 - h], r.cot.at[hs])]
    for u in range(3):
        loaded(u)
        gat.start(u)
    for i in range(3):
        swaps[i].start()
    for u in range(3, 9):
        loaded(u)
        gat.start(u)
        if u == 4:
            swaps[3].start()

    seg = r.seg_ids[pl.ds(h, 1), :]
    pad = r.pad_mask[pl.ds(h, 1), :]
    jj = lax.broadcasted_iota(jnp.int32, (KP, T), 0)
    tt = lax.broadcasted_iota(jnp.int32, (KP, T), 1)
    slot = jnp.sum(jnp.where(tt == 2 * jj, seg, 0), 1, keepdims=True)
    same = slot == seg
    r.smask[...] = jnp.where(same, 0.0, -1e30)
    r.keep[...] = jnp.where(same & (pad == 0), 1.0, 0.0).astype(BF16)
    gain_a, shift_a, b_out, gain_f, shift_f, b_down = (row_vec(v) for v in (r.attn_gain, r.attn_shift, r.b_out, r.ffn_gain, r.ffn_shift, r.b_down))
    for u, stage in ((0, 1), (1, 1), (0, 2), (2, 1), (1, 2), (0, 3), (2, 2)):
        gat.step(u, stage)

    loaded("x")
    swaps[0].wait()
    gat.step(1, 3)

    def ln1(rs):
        xh, _ = norm_stats(r.x[rs, :].astype(F32))
        r.nin[rs, :] = (xh * gain_a + shift_a).astype(BF16)
    blocks(T, 64, ln1)
    r.nint[...] = r.nin[...].T
    loaded("c")
    swaps[1].wait()
    swaps[2].wait()
    e = jnp.where(r.keep[...].astype(F32) > 0.5, r.comp[...].astype(F32), 0.0)
    r.e[...] = e.astype(BF16)
    r.et[...] = e.T.astype(BF16)

    def hook(i, table):
        for at, todo in sorted(table.items()):
            @pl.when(i == at)
            def _(todo=todo):
                for u, stage in todo:
                    gat.step(u, stage)
    fore = {0: [(2, 3)], 3: [(3, 1)], 4: [(4, 1)], 5: [(3, 2)]}

    def pair(i, carry):
        far = lax.div(i, 3)
        g = lax.rem(h + far, 2)
        pp = i - 3 * far

        @pl.when(far == 1)
        def _():
            gat.ready(pp, True)
        attn_forward(r, g * 3 + pp)
        hook(i, fore)
        return carry
    lax.fori_loop(0, 6, pair, 0)

    def proj(rs):
        o = nn(r.mix[0, rs, :], w_out(r, 0))
        for p in range(1, NP_):
            o = o + nn(r.mix[p, rs, :], w_out(r, p))
        res = r.x[rs, :].astype(F32) + (o + b_out)
        r.res[rs, :] = res
        xh, _ = norm_stats(res)
        r.nmid[rs, :] = (xh * gain_f + shift_f).astype(BF16)
        r.ffn[rs, :] = res + b_down
        r.dmid[rs, :] = jnp.zeros_like(res)
    blocks(T, 128, proj)
    r.nmidt[...] = r.nmid[...].T
    gat.step(4, 2)
    loaded("t")
    swaps[3].wait()

    lags = red.lags()

    def ticks(group):
        for j in range(SUB // 2):
            red.tick(group * (SUB // 2) + j, lags, False)

    late = {1: [(3, 3)], 2: [(4, 3), (5, 1), (6, 1)], 3: [(5, 2), (7, 1)], 4: [(6, 2), (8, 1)], 5: [(7, 2), (5, 3)], 6: [(8, 2)], 7: [(6, 3)],
            8: [(7, 3)], 9: [(8, 3)]}

    def main(i, carry):
        far = (1 - lax.rem(i, 2)) * jnp.minimum(i, 1) + lax.div(i, 11)
        k = lax.div(i + 1 - 2 * far, 2)

        @pl.when(far == 1)
        def _():
            gat.ready(3 + k, False)
        ffn_chunk(r, k, lax.rem(h + far, 2))
        hook(i, late)

        @pl.when(i > 1)
        def _():
            ticks(i - 2)
        return carry
    lax.fori_loop(0, 12, main, 0)

    r.vec[0] = jnp.zeros((16, D), F32)

    def ln2b(rs):
        xh, rstd = norm_stats(r.res[rs, :])
        dm = r.dmid[rs, :]
        cot = r.cot[rs, :].astype(F32)
        d = cot + norm_back(dm, xh, rstd, gain_f)
        r.res[rs, :] = d
        r.drl[rs, :] = d.astype(BF16)
        r.nmid[rs, :] = r.ffn[rs, :].astype(BF16)
        for i, v in ((2, d), (3, dm * xh), (4, dm), (5, cot)):
            r.vec[0, i:i + 1, :] += jnp.sum(v, 0, keepdims=True)
        r.dmid[rs, :] = jnp.zeros_like(d)
    blocks(T, 64, ln2b)
    ticks(10)
    r.dcomp[...] = jnp.zeros_like(r.dcomp)

    def back(i, carry):
        pp = lax.div(i, 2)
        g = lax.rem(h + i, 2)
        attn_backward(r, g * 3 + pp, g, 6 + pp)
        ticks(11 + i)
        return carry
    lax.fori_loop(0, 6, back, 0)
    gc = jnp.where(r.keep[...].astype(F32) > 0.5, r.dcomp[...], 0.0).astype(BF16)
    for g in range(2):
        for j in range(4):
            lo = (j % 2) * 128
            r.cgrad[j // 2, g, lo:lo + 128, :] = gc[g * 128:(g + 1) * 128, j * 128:(j + 1) * 128]

    def ln1b(rs):
        xh, rstd = norm_stats(r.x[rs, :].astype(F32))
        dn = r.dmid[rs, :]
        r.nin[rs, :] = (r.res[rs, :] + norm_back(dn, xh, rstd, gain_a)).astype(BF16)
        r.vec[0, 0:1, :] += jnp.sum(dn * xh, 0, keepdims=True)
        r.vec[0, 1:2, :] += jnp.sum(dn, 0, keepdims=True)
    blocks(T, 64, ln1b)
    for g in range(2):
        for i in range(2):
            at = 6 + g * 2 + i
            r.vec[0, at:at + 1, :] = jnp.concatenate([r.gbup[g * 6 + 3 * i + j] for j in range(3)], 1)
    for j in range(3):
        r.vec[0, 10 + j:11 + j, :] = jnp.concatenate([r.gbqkv[p][:, j * 128:(j + 1) * 128] for p in range(NP_)], 1)

    bits = [red.flip]
    s = 1
    while s < n:
        v = lax.rem(lax.div(b, s), 2)
        bits.append((b + s - 2 * s * v, h))
        s *= 2

    def vec_copy(i):
        return pltpu.make_async_remote_copy(src_ref=r.vec.at[i], dst_ref=r.vrecv.at[i], send_sem=r.vsend.at[i], recv_sem=r.vrsem.at[i],
                                            device_id=bits[i], device_id_type=MESH)

    def vec_step(i):
        if i > 0:
            vec_copy(i - 1).wait()
            r.vec[i] = r.vec[i - 1] + r.vrecv[i - 1]
        if i < len(bits):
            vec_copy(i).start()

    hs_far = pl.ds(pl.multiple_of((1 - h) * 256, 256), 256)
    backs = []
    for i, (src, dst) in enumerate(((r.nmid, r.out_y), (r.nin, r.out_ig))):
        backs.append(swap(4 + i, src.at[hs_far], dst.at[h]))
        dst[h] = src[hs, :]
    vec_step(0)
    first = 17 * (SUB // 2)
    stride = max(1, (TOTAL + lags[-1] - first) // (len(bits) + 1))
    for i in range(first, TOTAL + lags[-1] + 1):
        red.tick(i, lags, True)
        if i > first and (i - first) % stride == 0 and (i - first) // stride <= len(bits):
            vec_step((i - first) // stride)
        if i == TOTAL - 1 + lags[2]:
            for cp in backs:
                cp.start()
    r.out_vec[...] = r.vec[len(bits)]
    for cp in backs:
        cp.wait()


ARGS = ["inputs", "cotangent", "seg_ids", "pad_mask", "attn_gain", "attn_shift", "w_query", "w_key", "w_value", "b_query", "b_key", "b_value",
        "compress", "w_out", "b_out", "ffn_gain", "ffn_shift", "w_up", "b_up", "w_down", "b_down"]
IN_HBM = ["inputs", "cotangent", "w_query", "w_key", "w_value", "compress", "w_out", "w_up", "w_down"]


def run_layer(n, args):
    bits = n.bit_length()
    out = dict(out_y=((2, 256, D), BF16), out_ig=((2, 256, D), BF16), out_grad=((UNITS, 2, ROWS, 128), BF16), out_comp=((2, 256, 128), BF16), out_vec=((16, D), F32))
    scr = dict(x=((T, D), BF16), cot=((T, D), BF16), comp=((KP, T), BF16), bias=((18, 1, 384), F32), wa=((NP_, 1024, 384), BF16), wf=((NF, ROWS, 256), BF16),
               e=((KP, T), BF16), et=((T, KP), BF16), smask=((KP, T), F32), keep=((KP, T), BF16), nin=((T, D), BF16), nint=((D, T), BF16),
               qkv=((NP_, T, 384), BF16), kvc=((NP_, KP, 256), BF16), s=((512, T), F32), p=((NP_, 512, T), BF16), ds=((512, T), BF16),
               mixt=((NP_, 128, T), BF16), mix=((NP_, T, 128), BF16), res=((T, D), F32), nmid=((T, D), BF16), nmidt=((D, T), BF16),
               ffn=((T, D), F32), dmid=((T, D), F32), drl=((T, D), BF16), dcomp=((KP, T), F32),
               vec=((bits + 1, 16, D), F32), vrecv=((bits, 16, D), F32),
               gbup=((NF, 1, 256), F32), gbqkv=((NP_, 1, 384), F32), grad=((UNITS, 2, 2, ROWS, 128), BF16), cgrad=((2, 2, 256, 128), BF16))
    steps = len(orders(n)[0])
    for pre, rows in (("", PART), ("c", 256)):
        scr[pre + "rc"] = ((slots(0) if pre == "" else 1, 2, rows, 128), BF16)
        for i in range(steps):
            scr["%shalf%d" % (pre, i)] = ((slots(1 + i) if pre == "" else 1, max(landing(rows, order)[i] for order in orders(n)), 128), BF16)
    stages = 2 * steps + 1
    width = max(1 if order[0] == HEAD else 2 for order in orders(n))
    sems = dict(rsend=(stages, 2 * max(GAPS), width), rrecv=(stages, 2 * max(GAPS), width), gsend=(9, 4), grecv=(9, 4), ssend=(6,), srecv=(6,), vsend=(bits,), vrsem=(bits,),
                lsem=(48,))
    names = ARGS + list(out) + list(scr) + list(sems)
    hbm, vmem = pl.BlockSpec(memory_space=pl.ANY), pl.BlockSpec(memory_space=pltpu.VMEM)
    return pl.pallas_call(
        lambda *refs: layer(n, names, refs),
        out_shape=[pltpu.VMEM(*v) for v in out.values()],
        in_specs=[hbm if a in IN_HBM else vmem for a in ARGS], out_specs=[vmem] * len(out),
        scratch_shapes=[pltpu.VMEM(*v) for v in scr.values()] + [pltpu.SemaphoreType.DMA(v) for v in sems.values()],
        compiler_params=pltpu.CompilerParams(collective_id=0, has_side_effects=True, vmem_limit_bytes=53 * MIB), name="layer")(*args)


def finish(refs):
    (y_in, ig_in, g_in, c_in, v_in, y, ig, gain_a, shift_a, wq, wk, wv, bq, bk, bv, comp, wo, bo, gain_f, shift_f, wu, bu, wd, bd,
     fa, fo, fu, fd, fc, osem) = refs
    h = lax.axis_index("head")
    outs = iter(range(64))
    pend = []

    def put(src, dst):
        cp = pltpu.make_async_copy(src, dst, osem.at[next(outs)])
        cp.start()
        pend.append(cp)
    put(y_in, y)
    put(ig_in, ig)
    for i, o in enumerate((gain_a, shift_a, bo, gain_f, shift_f, bd)):
        o[...] = v_in[i, :]
    for i, o in enumerate((bq, bk, bv)):
        v = v_in[10 + i:11 + i, :]
        o[...] = jnp.where(h == 0, v[:, :384], v[:, 384:]).reshape(384)
    v = jnp.where(h == 0, v_in[6:8, :], v_in[8:10, :])
    bu[...] = jnp.concatenate([v[0:1], v[1:2]], 1).reshape(1536)
    for k in range(6):
        for ch in range(2):
            fu[k, :, ch * 128:(ch + 1) * 128] = g_in[k, ch, 0:768, :].astype(F32)
            for j in range(3):
                at = (ch * 3 + j) * 128
                fd[k, :, at:at + 128] = g_in[k, ch, 768 + j * 256:1024 + j * 256, :].astype(F32)
        put(fu.at[k], wu.at[:, k * 256:(k + 1) * 256])
        put(fd.at[k], wd.at[k * 256:(k + 1) * 256])
    for p in range(3):
        u = 6 + p
        for ch in range(2):
            for j in range(3):
                fa[j, ch * 384:(ch + 1) * 384, p * 128:(p + 1) * 128] = g_in[u, ch, j * 384:(j + 1) * 384, :].astype(F32)
                at = (ch * 3 + j) * 128
                fo[p, :, at:at + 128] = g_in[u, ch, 1152 + j * 128:1280 + j * 128, :].astype(F32)
        put(fo.at[p], wo.at[p * 128:(p + 1) * 128])
    for j, o in enumerate((wq, wk, wv)):
        put(fa.at[j], o)
    for j in range(4):
        fc[:, j * 128:(j + 1) * 128] = c_in[j // 2, (j % 2) * 128:(j % 2) * 128 + 128, :].astype(F32)
    put(fc, comp)
    for cp in pend:
        cp.wait()


def run_finish(parts):
    hbm, vmem = pl.BlockSpec(memory_space=pl.ANY), pl.BlockSpec(memory_space=pltpu.VMEM)
    f = lambda *s: jax.ShapeDtypeStruct(s, F32)
    row = jax.ShapeDtypeStruct((2, 256, D), BF16)
    outs = [(row, hbm), (row, hbm), (f(D), vmem), (f(D), vmem), (f(D, 384), hbm), (f(D, 384), hbm), (f(D, 384), hbm), (f(384), vmem), (f(384), vmem), (f(384), vmem),
            (f(128, T), hbm), (f(384, D), hbm), (f(D), vmem), (f(D), vmem), (f(D), vmem), (f(D, 1536), hbm), (f(1536), vmem), (f(1536, D), hbm), (f(D), vmem)]
    scr = [((3, D, 384), F32), ((3, 128, D), F32), ((6, D, 256), F32), ((6, 256, D), F32), ((128, T), F32)]
    return pl.pallas_call(
        lambda *refs: finish(refs), out_shape=[o for o, _ in outs], in_specs=[vmem] * 5, out_specs=[s for _, s in outs],
        scratch_shapes=[pltpu.VMEM(*v) for v in scr] + [pltpu.SemaphoreType.DMA((64,))],
        compiler_params=pltpu.CompilerParams(vmem_limit_bytes=40 * MIB), name="finish")(*parts)


def solution(mesh):
    n = mesh.shape["batch"]

    def on_device(*args):
        return tuple(run_finish(run_layer(n, args)))

    tok, rep, col, vec, row = P("batch", "head", None), P(), P(None, "head"), P("head"), P("head", None)
    ids = P("batch", None)
    return jax.shard_map(
        on_device, mesh=mesh,
        in_specs=(tok, tok, ids, ids, rep, rep, col, col, col, vec, vec, vec, row, row, rep, rep, rep, col, vec, row, rep),
        out_specs=(tok, tok, rep, rep, col, col, col, vec, vec, vec, row, row, rep, rep, rep, col, vec, row, rep),
        check_vma=False)
```

```python
import functools
import operator

import jax
import jax.numpy as jnp
from jax import lax
from jax.experimental import pallas as pl
from jax.experimental.pallas import tpu as pltpu
from jax.sharding import PartitionSpec as P

F32, BF16 = jnp.float32, jnp.bfloat16
T, D, KP = 512, 768, 256
NP_, NF = 6, 12
UNITS = 9
ROWS = 1536
SUB = 4
PART = ROWS // SUB
TOTAL = UNITS * SUB
EPS = 1e-5
SQRT_HALF = 0.7071067811865476
INV_SQRT_TWO_PI = 0.3989422804014327
MESH = pl.DeviceIdType.MESH
MIB = 1 << 20


def nn(a, b):
    return jnp.dot(a, b, preferred_element_type=F32)


def nt(a, b):
    return lax.dot_general(a, b, (((1,), (1,)), ((), ())), preferred_element_type=F32)


def norm_stats(v):
    mu = jnp.mean(v, -1, keepdims=True)
    c = v - mu
    rstd = lax.rsqrt(jnp.mean(c * c, -1, keepdims=True) + EPS)
    return c * rstd, rstd


def norm_back(g_out, xhat, rstd, gain):
    g = g_out * gain
    mg = jnp.mean(g, -1, keepdims=True)
    mp = jnp.mean(g * xhat, -1, keepdims=True)
    return rstd * (g - mg - xhat * mp)


def row_vec(ref):
    return ref[...].astype(F32).reshape(1, ref.shape[0])


def blocks(n, size, body):
    def step(i, carry):
        body(pl.ds(pl.multiple_of(i * size, size), size))
        return carry
    lax.fori_loop(0, n // size, step, 0)


class Refs:
    pass


HEAD = (0, 2)
GAPS = (2, 6, 4, 3, 3, 3, 6, 6, 5)
SLOTS = (5, 13, 11, 8, 7, 7, 13, 13, 11)


def turn(u, n):
    if len(orders(n)) == 1 or u % 2 or u < 12:
        return 0
    return 1 if u < 24 else 2


def gap(stage):
    return GAPS[min(stage, len(GAPS) - 1)]


def slots(stage):
    return SLOTS[min(stage, len(SLOTS) - 1)]


def orders(n):
    return {16: [(HEAD, (2, 2), (4, 2), (8, 2)), ((2, 2), HEAD, (4, 2), (8, 2)), (HEAD, (4, 2), (2, 2), (8, 2))], 128: [(HEAD, (2, 2), (4, 2), (16, 2), (8, 2), (32, 2), (64, 2))]}[n]


def landing(rows, order):
    out, both = [], 2
    for axis in order:
        if axis == HEAD:
            both = 1
            out.append(rows)
        else:
            rows = rows if rows % (8 * axis[1]) else rows // axis[1]
            out.append(both * (axis[1] - 1) * rows)
    return out


def copies(n):
    most = [max(axes[0][1] - 1 if i else 1 for axes in [(a,)]) for i, a in enumerate(orders(n)[0])]
    if len(orders(n)) > 1:
        most = [2 for _ in most]
    back = [axis[1] - 1 for axis in reversed(orders(n)[0]) if axis != HEAD]
    return [1, *most, *back, 1]


def places(n):
    out = [0]
    for stage, count in enumerate(copies(n)):
        out.append(out[-1] + slots(stage) * count)
    return out


def attn_forward(r, p):
    lane = lax.broadcasted_iota(jnp.int32, (KP, 128), 1) < 64
    row = lax.broadcasted_iota(jnp.int32, (128, KP), 0) < 64
    zero = jnp.zeros((), BF16)
    g = p // 3
    bias = r.bias[g * 9 + p - g * 3]
    qkv = (nn(r.nin[...], r.wa[p, 0:D, :]) + bias).astype(BF16)
    r.qkv[p] = qkv
    kvc = nn(r.e[...], qkv[:, 128:]).astype(BF16)
    r.kvc[p] = kvc
    kc = kvc[:, :128] * jnp.asarray(0.125, BF16)
    kst = jnp.concatenate([jnp.where(lane, kc, zero), jnp.where(lane, zero, kc)], 0)
    r.s[...] = nt(kst, qkv[:, :128])
    for h in range(2):
        for t in range(4):
            rs, ts = pl.ds(h * KP, KP), pl.ds(t * 128, 128)
            s = r.s[rs, ts] + r.smask[:, ts]
            m = jnp.max(s, 0, keepdims=True)
            e = jnp.exp(s - m)
            inv = 1.0 / jnp.sum(e, 0, keepdims=True)
            r.p[p, rs, ts] = (e * inv).astype(BF16)
    vt = kvc[:, 128:].T
    lhs = jnp.concatenate([jnp.where(row, vt, zero), jnp.where(row, zero, vt)], 1)
    mt = nn(lhs, r.p[p]).astype(BF16)
    r.mixt[p] = mt
    r.mix[p] = mt.T


def w_out(r, p):
    return jnp.concatenate([r.wa[p, 768:896, :], r.wa[p, 896:1024, :]], 1)


def attn_backward(r, p, g, unit):
    lane = lax.broadcasted_iota(jnp.int32, (KP, 128), 1) < 64
    row = lax.broadcasted_iota(jnp.int32, (128, KP), 0) < 64
    zero = jnp.zeros((), BF16)
    dm = r.mix[p]
    kvc = r.kvc[p]
    qkv = r.qkv[p]
    vc = kvc[:, 128:]
    vst = jnp.concatenate([jnp.where(lane, vc, zero), jnp.where(lane, zero, vc)], 0)
    r.s[...] = nt(vst, dm)
    for h in range(2):
        for t in range(4):
            rs, ts = pl.ds(h * KP, KP), pl.ds(t * 128, 128)
            pr = r.p[p, rs, ts].astype(F32)
            dp = r.s[rs, ts]
            c = jnp.sum(pr * dp, 0, keepdims=True)
            r.ds[rs, ts] = (pr * (dp - c)).astype(BF16)
    dvs = nn(r.p[p], dm)
    dks = nn(r.ds[...], qkv[:, :128]) * 0.125
    dkv = jnp.concatenate([jnp.where(lane, dks[:KP], dks[KP:]), jnp.where(lane, dvs[:KP], dvs[KP:])], 1).astype(BF16)
    kt = (kvc[:, :128] * jnp.asarray(0.125, BF16)).T
    lhs = jnp.concatenate([jnp.where(row, kt, zero), jnp.where(row, zero, kt)], 1)
    dq = nn(lhs, r.ds[...]).astype(BF16).T
    dkvt = nn(r.et[...], dkv).astype(BF16)
    r.dcomp[...] += nt(dkv, qkv[:, 128:])
    dqkv = jnp.concatenate([dq, dkvt], 1)
    gw = nn(r.nint[...], dqkv).astype(BF16)
    for j in range(3):
        for ch in range(2):
            r.grad[unit, ch, g, j * 384:(j + 1) * 384, :] = gw[ch * 384:(ch + 1) * 384, j * 128:(j + 1) * 128]
    r.gbqkv[p] = jnp.sum(dqkv.astype(F32), 0, keepdims=True)
    r.dmid[...] += nt(dqkv, r.wa[p, 0:D, :])


def out_backward(r):
    for p in range(0, NP_, 2):
        dm = nt(r.drl[...], jnp.concatenate([w_out(r, p), w_out(r, p + 1)], 0)).astype(BF16)
        r.mix[p] = dm[:, :128]
        r.mix[p + 1] = dm[:, 128:]
    gw = nn(jnp.concatenate([r.mixt[p] for p in range(NP_)], 0), r.drl[...]).astype(BF16)
    for p in range(NP_):
        for j in range(6):
            lo = 1152 + (j % 3) * 128
            r.grad[6 + p % 3, j // 3, p // 3, lo:lo + 128, :] = gw[p * 128:(p + 1) * 128, j * 128:(j + 1) * 128]


def ffn_chunk(r, k, g):
    c = g * 6 + k
    wup = r.wf[c, 0:D, :]
    wdn = jnp.concatenate([r.wf[c, 768 + 256 * j:1024 + 256 * j, :] for j in range(3)], 1)
    bup = r.bias[g * 9 + 3 + k][:, :256]
    r.s[:, 0:256] = nn(r.nmid[...], wup)
    r.s[:, 256:512] = nt(r.cot[...], wdn)
    for i in range(8):
        rs = pl.ds(i * 64, 64)
        pre = r.s[rs, 0:256] + bup
        phi = 0.5 * (1.0 + lax.erf(pre * SQRT_HALF))
        pdf = jnp.exp(-0.5 * pre * pre) * INV_SQRT_TWO_PI
        r.ds[rs, 0:256] = (pre * phi).astype(BF16)
        r.ds[rs, 256:512] = (r.s[rs, 256:512] * (phi + pre * pdf)).astype(BF16)
    r.ffn[...] += nn(r.ds[:, 0:256], wdn)
    r.dmid[...] += nt(r.ds[:, 256:512], wup)
    gw = nn(r.ds[:, 0:256].T, r.cot[...]).astype(BF16)
    for j in range(6):
        lo = 768 + (j % 3) * 256
        r.grad[k, j // 3, g, lo:lo + 256, :] = gw[:, j * 128:(j + 1) * 128]
    gw = nn(r.nmidt[...], r.ds[:, 256:512]).astype(BF16)
    for ch in range(2):
        r.grad[k, ch, g, 0:768, :] = gw[:, ch * 128:(ch + 1) * 128]
    r.gbup[c] = jnp.sum(r.ds[:, 256:512].astype(F32), 0, keepdims=True)


def add_rows(dst, srcs, out=None):
    out = dst if out is None else out
    n = dst.shape[0]
    for lo in range(0, n, 384):
        rows = pl.ds(lo, min(384, n - lo))
        if len(srcs) == 1:
            out[rows, :] = dst[rows, :] + srcs[0][rows, :]
        else:
            out[rows, :] = functools.reduce(operator.add, [v[rows, :].astype(F32) for v in srcs], dst[rows, :].astype(F32)).astype(BF16)


def part_of(u):
    if isinstance(u, int):
        return u // SUB, pl.ds(u % SUB * PART, PART)
    return lax.div(u, SUB), pl.ds(pl.multiple_of(lax.rem(u, SUB) * PART, PART), PART)


class Reduce:
    def __init__(self, r, n):
        self.r = r
        b, h = lax.axis_index("batch"), lax.axis_index("head")
        self.b, self.h, self.c = b, h, lax.rem(b, 2)
        self.core = (b + 1 - 2 * self.c, h)
        self.flip = (b, 1 - h)
        self.orders = orders(n)
        self.families = len(self.orders)
        self.copies, self.places = copies(n), places(n)
        self.turn = lambda u: turn(u, n)

    def bit(self, stride):
        return lax.rem(lax.div(self.b, stride), 2)

    def across(self, stride):
        return (self.b + stride - 2 * stride * self.bit(stride), self.h)

    def peers(self, axis):
        if axis == HEAD:
            return self.h, [(1 - self.h, self.flip)]
        stride, size = axis
        a = lax.rem(lax.div(self.b, stride), size)
        if size == 2:
            return a, [(1 - a, self.across(stride))]
        ks = [lax.rem(a + j, size) for j in range(1, size)]
        return a, [(k, (self.b + (k - a) * stride, self.h)) for k in ks]

    def copy(self, src, dst, stage, u, dev, j=0):
        at = self.places[stage] + lax.rem(u, slots(stage)) * self.copies[stage] + j
        return lambda: pltpu.make_async_remote_copy(src_ref=src, dst_ref=dst, send_sem=self.r.rsend.at[at], recv_sem=self.r.rrecv.at[at],
                                                    device_id=dev, device_id_type=MESH)

    def exchanges(self, u, family, bufs):
        grad, rc, halves, fin = bufs
        one = rc.shape[0] == 1
        h, c, order = self.h, self.c, self.orders[family]
        slot = 0 if one else lax.rem(u, slots(0))
        none = lambda: None

        def core_add():
            for g in range(2):
                add_rows(grad.at[c, g], [rc.at[slot, g]])
        stages = [([self.copy(grad.at[1 - c], rc.at[slot], 0, u, self.core)], core_add)]
        base, part, both, gathers = 0, grad.shape[2], True, []
        for i, axis in enumerate(order):
            buf, last = halves[i], i == len(order) - 1
            place, others = self.peers(axis)
            if axis == HEAD or part % (8 * axis[1]):
                rows = pl.ds(base, part)
                sends = [(rows, dev) for _, dev in others]
            else:
                part //= axis[1]
                sends = [(pl.ds(pl.multiple_of(base + k * part, part), part), dev) for k, dev in others]
                base = pl.multiple_of(base + place * part, part)
                rows = pl.ds(base, part)
                gathers.append((axis, base, part))
            if axis == HEAD:
                both = False
                moves = [(1 - h, h)]
            else:
                moves = [(0, 0), (1, 1)] if both else [(h, h)]
            cps, adds = [], []
            for give, keep in moves:
                lands = []
                for send, dev in sends:
                    land = buf.at[0 if one else lax.rem(u, slots(1 + i)), pl.ds(len(cps) * part, part)]
                    cps.append(self.copy(grad.at[c, give, send], land, 1 + i, u, dev, len(cps)))
                    lands.append(land)
                adds.append((keep, lands))

            def add(adds=adds, rows=rows, last=last):
                for g, lands in adds:
                    add_rows(grad.at[c, g, rows], lands, fin.at[c, rows] if last else None)
            stages.append((cps, add))
        for axis, lo, count in reversed(gathers):
            own = fin.at[c, pl.ds(lo, count)]
            stages.append(([self.copy(own, own, len(stages), u, dev, j) for j, (_, dev) in enumerate(self.peers(axis)[1])], none))
        stages.append(([self.copy(fin.at[c], fin.at[c], len(stages), u, self.core)], none))
        return stages

    def lags(self):
        count = len(self.exchanges(0, 0, self.bufs(0)))
        out = [0]
        for i in range(count):
            out.append(out[-1] + gap(i))
        return out

    def small(self):
        r = self.r
        return (r.cgrad, r.crc, r.chalves, r.out_comp)

    def bufs(self, u):
        r = self.r
        at, rows = part_of(u)
        return (r.grad.at[at, :, :, rows], r.rc, r.halves, r.out_grad.at[at, :, rows])

    def step(self, u, i, family, bufs):
        st = self.exchanges(u, family, bufs)
        if i > len(st):
            return
        if i > 0:
            for cp in st[i - 1][0]:
                cp().wait()
            st[i - 1][1]()
        if i < len(st):
            for cp in st[i][0]:
                cp().start()

    def tick(self, i, lags, static):
        for s in reversed(range(len(lags))):
            u = i - lags[s]
            if static:
                if 0 <= u < TOTAL:
                    self.step(u, s, self.turn(u), self.bufs(u))
                elif u == TOTAL:
                    self.step(u, s, 0, self.small())
                continue
            if s == 0:
                @pl.when((u >= 0) & (u < TOTAL))
                def _(s=s, u=u):
                    self.step(u, s, 0, self.bufs(u))
                continue
            for f in range(self.families):
                even = lax.rem(u, 2) == 0
                here = u >= 0
                if self.families > 1:
                    here = ((u < 12) | jnp.logical_not(even), even & (u >= 12) & (u < 24), even & (u >= 24))[f]

                @pl.when((u >= 0) & (u < TOTAL) & here)
                def _(s=s, u=u, f=f):
                    self.step(u, s, f, self.bufs(u))


class Gather:
    def __init__(self, r, red):
        self.r = r
        self.h = red.h
        c, x, z = red.bit(1), red.bit(2), red.bit(4)
        self.q = (c * 4 + z * 2 + x, c * 4 + x * 2 + z)
        self.dev = [(red.flip, red.across(2), red.across(4), red.core), (red.flip, red.across(4), red.across(2), red.core)]

    def copy(self, u, stage, attn, odd):
        h = self.h
        g = h if stage == 0 else 1 - h
        unit = self.r.wa.at[g * 3 + u] if attn else self.r.wf.at[g * 6 + u - 3]
        piece = unit.shape[0] // 8
        count = 1 if stage == 0 else 1 << (stage - 1)
        lo = lax.div(self.q[odd], count) * count * piece
        view = unit.at[pl.ds(pl.multiple_of(lo, piece), count * piece)]
        return pltpu.make_async_remote_copy(src_ref=view, dst_ref=view, send_sem=self.r.gsend.at[u, stage], recv_sem=self.r.grecv.at[u, stage],
                                            device_id=self.dev[odd][stage], device_id_type=MESH)

    def start(self, u):
        self.copy(u, 0, u < 3, u % 2).start()

    def step(self, u, stage):
        self.copy(u, stage - 1, u < 3, u % 2).wait()
        if stage < 4:
            self.copy(u, stage, u < 3, u % 2).start()

    def ready(self, u, attn):
        for odd in range(2):
            @pl.when(lax.rem(u, 2) == odd)
            def _(odd=odd):
                self.copy(u, 3, attn, odd).wait()


def layer(n, names, refs):
    r = Refs()
    for name, ref in zip(names, refs):
        setattr(r, name, ref)
    steps = len(orders(n)[0])
    r.halves = [getattr(r, "half%d" % i) for i in range(steps)]
    r.chalves = [getattr(r, "chalf%d" % i) for i in range(steps)]
    red = Reduce(r, n)
    gat = Gather(r, red)
    b, h = red.b, red.h

    barrier = pltpu.get_barrier_semaphore()
    peers = [red.core] + [dev for axis in red.orders[0] for _, dev in red.peers(axis)[1]]
    for dev in peers:
        pl.semaphore_signal(barrier, inc=1, device_id=dev, device_id_type=MESH)

    hs = pl.ds(pl.multiple_of(h * 256, 256), 256)
    cs = pl.ds(pl.multiple_of(h * 128, 128), 128)
    homes = [r.wa.at[h * 3 + u] for u in range(3)] + [r.wf.at[h * 6 + k] for k in range(6)] + [r.x.at[hs], r.comp.at[cs], r.cot.at[hs]]

    def load(key, src, dst):
        pltpu.make_async_copy(src, dst, r.lsem.at[key]).start()

    def loaded(key):
        pltpu.make_async_copy(homes[key], homes[key], r.lsem.at[key]).wait()

    def swap(i, src, dst):
        return pltpu.make_async_remote_copy(src_ref=src, dst_ref=dst, send_sem=r.ssend.at[i], recv_sem=r.srecv.at[i],
                                            device_id=red.flip, device_id_type=MESH)
    quarter = pl.ds(pl.multiple_of(h * 128 + red.c * 64, 64), 64)
    far_quarter = pl.ds(pl.multiple_of((1 - h) * 128 + red.c * 64, 64), 64)
    share = pltpu.make_async_remote_copy(src_ref=r.comp.at[far_quarter], dst_ref=r.comp.at[far_quarter], send_sem=r.ssend.at[6], recv_sem=r.srecv.at[6],
                                         device_id=red.core, device_id_type=MESH)
    bs = r.bias.at[pl.ds(h * 9, 9)]
    swaps = [swap(0, r.inputs.at[1 - h], r.x.at[hs]), swap(1, r.compress.at[pl.ds(pl.multiple_of(red.c * 64, 64), 64)], r.comp.at[quarter]), swap(2, bs, bs),
             swap(3, r.cotangent.at[1 - h], r.cot.at[hs])]
    for u in range(3):
        unit, cols = r.wa.at[h * 3 + u], pl.ds(u * 128, 128)
        for j, w in enumerate((r.w_query, r.w_key, r.w_value)):
            load(u, w.at[:, cols], unit.at[0:768, j * 128:(j + 1) * 128])
        for j in range(2):
            load(u, r.w_out.at[cols, j * 384:(j + 1) * 384], unit.at[768 + 128 * j:896 + 128 * j])
    pl.semaphore_wait(barrier, len(peers))
    for u in range(3):
        loaded(u)
        gat.start(u)
    swaps[1].start()
    swaps[0].start()
    load(9, r.inputs.at[h], r.x.at[hs])
    load(10, r.compress, r.comp.at[cs])
    for k in range(6):
        unit = r.wf.at[h * 6 + k]
        load(3 + k, r.w_up.at[:, k * 256:(k + 1) * 256], unit.at[0:768])
        for j in range(3):
            load(3 + k, r.w_down.at[k * 256:(k + 1) * 256, j * 256:(j + 1) * 256], unit.at[768 + 256 * j:1024 + 256 * j])
    load(11, r.cotangent.at[h], r.cot.at[hs])
    bqkv = [row_vec(v) for v in (r.b_query, r.b_key, r.b_value)]
    bup = row_vec(r.b_up)
    for u in range(3):
        r.bias[h * 9 + u] = jnp.concatenate([v[:, u * 128:(u + 1) * 128] for v in bqkv], 1)
    for k in range(6):
        r.bias[h * 9 + 3 + k, :, 0:256] = bup[:, k * 256:(k + 1) * 256]
        r.bias[h * 9 + 3 + k, :, 256:384] = jnp.zeros((1, 128), F32)
    swaps[2].start()
    for u in range(3, 9):
        loaded(u)
        gat.start(u)
        if u == 4:
            swaps[3].start()

    seg = r.seg_ids[pl.ds(h, 1), :]
    pad = r.pad_mask[pl.ds(h, 1), :]
    jj = lax.broadcasted_iota(jnp.int32, (KP, T), 0)
    tt = lax.broadcasted_iota(jnp.int32, (KP, T), 1)
    slot = jnp.sum(jnp.where(tt == 2 * jj, seg, 0), 1, keepdims=True)
    same = slot == seg
    r.smask[...] = jnp.where(same, 0.0, -1e30)
    r.keep[...] = jnp.where(same & (pad == 0), 1.0, 0.0).astype(BF16)
    gain_a, shift_a, b_out, gain_f, shift_f, b_down = (row_vec(v) for v in (r.attn_gain, r.attn_shift, r.b_out, r.ffn_gain, r.ffn_shift, r.b_down))
    for u, stage in ((0, 1), (1, 1), (0, 2), (2, 1), (1, 2)):
        gat.step(u, stage)
    swaps[1].wait()
    share.start()
    gat.step(0, 3)
    gat.step(2, 2)

    loaded(9)
    swaps[0].wait()
    gat.step(1, 3)

    def ln1(rs):
        xh, _ = norm_stats(r.x[rs, :].astype(F32))
        r.nin[rs, :] = (xh * gain_a + shift_a).astype(BF16)
    blocks(T, 64, ln1)
    r.nint[...] = r.nin[...].T
    loaded(10)
    share.wait()
    swaps[2].wait()
    e = jnp.where(r.keep[...].astype(F32) > 0.5, r.comp[...].astype(F32), 0.0)
    r.e[...] = e.astype(BF16)
    r.et[...] = e.T.astype(BF16)

    def hook(i, table):
        for at, todo in sorted(table.items()):
            @pl.when(i == at)
            def _(todo=todo):
                for u, stage in todo:
                    gat.step(u, stage)
    fore = {0: [(2, 3)], 1: [(3, 1)], 3: [(4, 1)], 4: [(3, 2)], 5: [(4, 2)]}

    def pair(i, carry):
        far = lax.div(i, 3)
        g = lax.rem(h + far, 2)
        pp = i - 3 * far

        @pl.when(far == 1)
        def _():
            gat.ready(pp, True)
        attn_forward(r, g * 3 + pp)
        hook(i, fore)
        return carry
    lax.fori_loop(0, 6, pair, 0)

    r.res[...] = nn(jnp.concatenate([r.mix[p] for p in range(NP_)], 1), jnp.concatenate([w_out(r, p) for p in range(NP_)], 0))

    def proj(rs):
        res = r.x[rs, :].astype(F32) + (r.res[rs, :] + b_out)
        r.res[rs, :] = res
        xh, _ = norm_stats(res)
        r.nmid[rs, :] = (xh * gain_f + shift_f).astype(BF16)
        r.ffn[rs, :] = res + b_down
        r.dmid[rs, :] = jnp.zeros_like(res)
    blocks(T, 64, proj)
    r.nmidt[...] = r.nmid[...].T
    loaded(11)
    swaps[3].wait()

    lags = red.lags()

    def ticks(group):
        for j in range(SUB // 2):
            red.tick(group * (SUB // 2) + j, lags, False)

    late = {0: [(3, 3)], 1: [(4, 3)], 2: [(5, 1), (6, 1)], 3: [(5, 2), (7, 1)], 4: [(6, 2), (8, 1)], 5: [(7, 2), (5, 3)], 6: [(8, 2)], 7: [(6, 3)],
            8: [(7, 3)], 9: [(8, 3)]}

    def main(i, carry):
        far = (1 - lax.rem(i, 2)) * jnp.minimum(i, 1) + lax.div(i, 11)
        k = lax.div(i + 1 - 2 * far, 2)

        @pl.when(far == 1)
        def _():
            gat.ready(3 + k, False)
        ffn_chunk(r, k, lax.rem(h + far, 2))
        hook(i, late)

        @pl.when(i > 1)
        def _():
            ticks(i - 2)
        return carry
    lax.fori_loop(0, 12, main, 0)

    r.vec[0] = jnp.zeros((16, D), F32)

    def ln2b(rs):
        xh, rstd = norm_stats(r.res[rs, :])
        dm = r.dmid[rs, :]
        cot = r.cot[rs, :].astype(F32)
        d = cot + norm_back(dm, xh, rstd, gain_f)
        r.res[rs, :] = d
        r.drl[rs, :] = d.astype(BF16)
        r.nmid[rs, :] = r.ffn[rs, :].astype(BF16)
        for i, v in ((2, d), (3, dm * xh), (4, dm), (5, cot)):
            r.vec[0, i:i + 1, :] += jnp.sum(v, 0, keepdims=True)
        r.dmid[rs, :] = jnp.zeros_like(d)
    blocks(T, 64, ln2b)
    ticks(10)
    r.dcomp[...] = jnp.zeros_like(r.dcomp)
    out_backward(r)

    def back(i, carry):
        pp = lax.div(i, 2)
        g = lax.rem(h + i, 2)
        attn_backward(r, g * 3 + pp, g, 6 + pp)
        ticks(11 + i)
        return carry
    lax.fori_loop(0, 6, back, 0)
    gc = jnp.where(r.keep[...].astype(F32) > 0.5, r.dcomp[...], 0.0).astype(BF16)
    for g in range(2):
        for j in range(4):
            lo = (j % 2) * 128
            r.cgrad[j // 2, g, lo:lo + 128, :] = gc[g * 128:(g + 1) * 128, j * 128:(j + 1) * 128]

    def ln1b(rs):
        xh, rstd = norm_stats(r.x[rs, :].astype(F32))
        dn = r.dmid[rs, :]
        r.nin[rs, :] = (r.res[rs, :] + norm_back(dn, xh, rstd, gain_a)).astype(BF16)
        r.vec[0, 0:1, :] += jnp.sum(dn * xh, 0, keepdims=True)
        r.vec[0, 1:2, :] += jnp.sum(dn, 0, keepdims=True)
    blocks(T, 64, ln1b)
    for g in range(2):
        for i in range(2):
            at = 6 + g * 2 + i
            r.vec[0, at:at + 1, :] = jnp.concatenate([r.gbup[g * 6 + 3 * i + j] for j in range(3)], 1)
    for j in range(3):
        r.vec[0, 10 + j:11 + j, :] = jnp.concatenate([r.gbqkv[p][:, j * 128:(j + 1) * 128] for p in range(NP_)], 1)

    bits = [red.flip]
    s = 1
    while s < n:
        v = lax.rem(lax.div(b, s), 2)
        bits.append((b + s - 2 * s * v, h))
        s *= 2

    def vec_copy(i):
        return pltpu.make_async_remote_copy(src_ref=r.vec.at[i], dst_ref=r.vrecv.at[i], send_sem=r.vsend.at[i], recv_sem=r.vrsem.at[i],
                                            device_id=bits[i], device_id_type=MESH)

    def vec_step(i):
        if i > 0:
            vec_copy(i - 1).wait()
            r.vec[i] = r.vec[i - 1] + r.vrecv[i - 1]
        if i < len(bits):
            vec_copy(i).start()

    hs_far = pl.ds(pl.multiple_of((1 - h) * 256, 256), 256)
    backs = []
    for i, (src, dst) in enumerate(((r.nmid, r.out_y), (r.nin, r.out_ig))):
        backs.append(swap(4 + i, src.at[hs_far], dst.at[h]))
        dst[h] = src[hs, :]
    vec_step(0)
    first = 17 * (SUB // 2)
    stride = max(1, (TOTAL + lags[-1] - first) // (len(bits) + 1))
    for i in range(first, TOTAL + lags[-1] + 1):
        red.tick(i, lags, True)
        if i > first and (i - first) % stride == 0 and (i - first) // stride <= len(bits):
            vec_step((i - first) // stride)
        if i == TOTAL - 1 + lags[2]:
            for cp in backs:
                cp.start()
    r.out_vec[...] = r.vec[len(bits)]
    for cp in backs:
        cp.wait()


ARGS = ["inputs", "cotangent", "seg_ids", "pad_mask", "attn_gain", "attn_shift", "w_query", "w_key", "w_value", "b_query", "b_key", "b_value",
        "compress", "w_out", "b_out", "ffn_gain", "ffn_shift", "w_up", "b_up", "w_down", "b_down"]
IN_HBM = ["inputs", "cotangent", "w_query", "w_key", "w_value", "compress", "w_out", "w_up", "w_down"]


def run_layer(n, args):
    bits = n.bit_length()
    out = dict(out_y=((2, 256, D), BF16), out_ig=((2, 256, D), BF16), out_grad=((UNITS, 2, ROWS, 128), BF16), out_comp=((2, 256, 128), BF16), out_vec=((16, D), F32))
    scr = dict(x=((T, D), BF16), cot=((T, D), BF16), comp=((KP, T), BF16), bias=((18, 1, 384), F32), wa=((NP_, 1024, 384), BF16), wf=((NF, ROWS, 256), BF16),
               e=((KP, T), BF16), et=((T, KP), BF16), smask=((KP, T), F32), keep=((KP, T), BF16), nin=((T, D), BF16), nint=((D, T), BF16),
               qkv=((NP_, T, 384), BF16), kvc=((NP_, KP, 256), BF16), s=((512, T), F32), p=((NP_, 512, T), BF16), ds=((512, T), BF16),
               mixt=((NP_, 128, T), BF16), mix=((NP_, T, 128), BF16), res=((T, D), F32), nmid=((T, D), BF16), nmidt=((D, T), BF16),
               ffn=((T, D), F32), dmid=((T, D), F32), drl=((T, D), BF16), dcomp=((KP, T), F32),
               vec=((bits + 1, 16, D), F32), vrecv=((bits, 16, D), F32),
               gbup=((NF, 1, 256), F32), gbqkv=((NP_, 1, 384), F32), grad=((UNITS, 2, 2, ROWS, 128), BF16), cgrad=((2, 2, 256, 128), BF16))
    steps = len(orders(n)[0])
    for pre, rows in (("", PART), ("c", 256)):
        scr[pre + "rc"] = ((slots(0) if pre == "" else 1, 2, rows, 128), BF16)
        for i in range(steps):
            scr["%shalf%d" % (pre, i)] = ((slots(1 + i) if pre == "" else 1, max(landing(rows, order)[i] for order in orders(n)), 128), BF16)
    sems = dict(rsend=(places(n)[-1],), rrecv=(places(n)[-1],), gsend=(9, 4), grecv=(9, 4), ssend=(7,), srecv=(7,), vsend=(bits,), vrsem=(bits,),
                lsem=(12,))
    names = ARGS + list(out) + list(scr) + list(sems)
    hbm, vmem = pl.BlockSpec(memory_space=pl.ANY), pl.BlockSpec(memory_space=pltpu.VMEM)
    return pl.pallas_call(
        lambda *refs: layer(n, names, refs),
        out_shape=[pltpu.VMEM(*v) for v in out.values()],
        in_specs=[hbm if a in IN_HBM else vmem for a in ARGS], out_specs=[vmem] * len(out),
        scratch_shapes=[pltpu.VMEM(*v) for v in scr.values()] + [pltpu.SemaphoreType.DMA(v) for v in sems.values()],
        compiler_params=pltpu.CompilerParams(collective_id=0, has_side_effects=True, vmem_limit_bytes=55 * MIB), name="layer")(*args)


def finish(refs):
    (y_in, ig_in, g_in, c_in, v_in, y, ig, gain_a, shift_a, wq, wk, wv, bq, bk, bv, comp, wo, bo, gain_f, shift_f, wu, bu, wd, bd,
     fa, fo, fu, fd, fc, osem) = refs
    h = lax.axis_index("head")
    outs = iter(range(64))
    pend = []

    def put(src, dst):
        cp = pltpu.make_async_copy(src, dst, osem.at[next(outs)])
        cp.start()
        pend.append(cp)
    put(y_in, y)
    put(ig_in, ig)
    for i, o in enumerate((gain_a, shift_a, bo, gain_f, shift_f, bd)):
        o[...] = v_in[i, :]
    for i, o in enumerate((bq, bk, bv)):
        v = v_in[10 + i:11 + i, :]
        o[...] = jnp.where(h == 0, v[:, :384], v[:, 384:]).reshape(384)
    v = jnp.where(h == 0, v_in[6:8, :], v_in[8:10, :])
    bu[...] = jnp.concatenate([v[0:1], v[1:2]], 1).reshape(1536)
    for k in range(6):
        for ch in range(2):
            fu[k, :, ch * 128:(ch + 1) * 128] = g_in[k, ch, 0:768, :].astype(F32)
            for j in range(3):
                at = (ch * 3 + j) * 128
                fd[k, :, at:at + 128] = g_in[k, ch, 768 + j * 256:1024 + j * 256, :].astype(F32)
        put(fu.at[k], wu.at[:, k * 256:(k + 1) * 256])
        put(fd.at[k], wd.at[k * 256:(k + 1) * 256])
    for p in range(3):
        u = 6 + p
        for ch in range(2):
            for j in range(3):
                fa[j, ch * 384:(ch + 1) * 384, p * 128:(p + 1) * 128] = g_in[u, ch, j * 384:(j + 1) * 384, :].astype(F32)
                at = (ch * 3 + j) * 128
                fo[p, :, at:at + 128] = g_in[u, ch, 1152 + j * 128:1280 + j * 128, :].astype(F32)
        put(fo.at[p], wo.at[p * 128:(p + 1) * 128])
    for j, o in enumerate((wq, wk, wv)):
        put(fa.at[j], o)
    for j in range(4):
        fc[:, j * 128:(j + 1) * 128] = c_in[j // 2, (j % 2) * 128:(j % 2) * 128 + 128, :].astype(F32)
    put(fc, comp)
    for cp in pend:
        cp.wait()


def run_finish(parts):
    hbm, vmem = pl.BlockSpec(memory_space=pl.ANY), pl.BlockSpec(memory_space=pltpu.VMEM)
    f = lambda *s: jax.ShapeDtypeStruct(s, F32)
    row = jax.ShapeDtypeStruct((2, 256, D), BF16)
    outs = [(row, hbm), (row, hbm), (f(D), vmem), (f(D), vmem), (f(D, 384), hbm), (f(D, 384), hbm), (f(D, 384), hbm), (f(384), vmem), (f(384), vmem), (f(384), vmem),
            (f(128, T), hbm), (f(384, D), hbm), (f(D), vmem), (f(D), vmem), (f(D), vmem), (f(D, 1536), hbm), (f(1536), vmem), (f(1536, D), hbm), (f(D), vmem)]
    scr = [((3, D, 384), F32), ((3, 128, D), F32), ((6, D, 256), F32), ((6, 256, D), F32), ((128, T), F32)]
    return pl.pallas_call(
        lambda *refs: finish(refs), out_shape=[o for o, _ in outs], in_specs=[vmem] * 5, out_specs=[s for _, s in outs],
        scratch_shapes=[pltpu.VMEM(*v) for v in scr] + [pltpu.SemaphoreType.DMA((64,))],
        compiler_params=pltpu.CompilerParams(vmem_limit_bytes=40 * MIB), name="finish")(*parts)


def solution(mesh):
    n = mesh.shape["batch"]

    def on_device(*args):
        return tuple(run_finish(run_layer(n, args)))

    tok, rep, col, vec, row = P("batch", "head", None), P(), P(None, "head"), P("head"), P("head", None)
    ids = P("batch", None)
    return jax.shard_map(
        on_device, mesh=mesh,
        in_specs=(tok, tok, ids, ids, rep, rep, col, col, col, vec, vec, vec, row, row, rep, rep, rep, col, vec, row, rep),
        out_specs=(tok, tok, rep, rep, col, col, col, vec, vec, vec, row, row, rep, rep, rep, col, vec, row, rep),
        check_vma=False)
```

```python
import functools
import operator

import jax
import jax.numpy as jnp
from jax import lax
from jax.experimental import pallas as pl
from jax.experimental.pallas import tpu as pltpu
from jax.sharding import PartitionSpec as P

F32, BF16 = jnp.float32, jnp.bfloat16
T, D, KP = 512, 768, 256
NP_, NF = 6, 12
UNITS = 9
ROWS = 1536
SUB = 4
PART = ROWS // SUB
TOTAL = UNITS * SUB
EPS = 1e-5
SQRT_HALF = 0.7071067811865476
INV_SQRT_TWO_PI = 0.3989422804014327
MESH = pl.DeviceIdType.MESH
MIB = 1 << 20


def nn(a, b):
    return jnp.dot(a, b, preferred_element_type=F32)


def nt(a, b):
    return lax.dot_general(a, b, (((1,), (1,)), ((), ())), preferred_element_type=F32)


def norm_stats(v):
    mu = jnp.mean(v, -1, keepdims=True)
    c = v - mu
    rstd = lax.rsqrt(jnp.mean(c * c, -1, keepdims=True) + EPS)
    return c * rstd, rstd


def norm_back(g_out, xhat, rstd, gain):
    g = g_out * gain
    mg = jnp.mean(g, -1, keepdims=True)
    mp = jnp.mean(g * xhat, -1, keepdims=True)
    return rstd * (g - mg - xhat * mp)


def row_vec(ref):
    return ref[...].astype(F32).reshape(1, ref.shape[0])


def blocks(n, size, body):
    def step(i, carry):
        body(pl.ds(pl.multiple_of(i * size, size), size))
        return carry
    lax.fori_loop(0, n // size, step, 0)


class Refs:
    pass


HEAD = (0, 2)
GAPS = (2, 6, 4, 3, 3, 3, 6, 6, 5)
SLOTS = (5, 13, 11, 8, 7, 7, 13, 13, 11)


def turn(u, n):
    if len(orders(n)) == 1 or u % 2 or u < 12:
        return 0
    return 1 if u < 24 else 2


def gap(stage):
    return GAPS[min(stage, len(GAPS) - 1)]


def slots(stage):
    return SLOTS[min(stage, len(SLOTS) - 1)]


def orders(n):
    return {16: [(HEAD, (2, 2), (4, 2), (8, 2)), ((2, 2), HEAD, (4, 2), (8, 2)), (HEAD, (4, 2), (2, 2), (8, 2))], 128: [(HEAD, (2, 2), (4, 2), (16, 2), (8, 2), (32, 2), (64, 2))]}[n]


def landing(rows, order):
    out, both = [], 2
    for axis in order:
        if axis == HEAD:
            both = 1
            out.append(rows)
        else:
            rows = rows if rows % (8 * axis[1]) else rows // axis[1]
            out.append(both * (axis[1] - 1) * rows)
    return out


def copies(n):
    most = []
    for stage in range(len(orders(n)[0])):
        counts = []
        for order in orders(n):
            both = 2 if HEAD not in order[:stage + 1] else 1
            counts.append(both * (order[stage][1] - 1))
        most.append(max(counts))
    back = [axis[1] - 1 for axis in reversed(orders(n)[0]) if axis != HEAD]
    return [1, *most, *back, 1]


def places(n):
    out = [0]
    for stage, count in enumerate(copies(n)):
        out.append(out[-1] + slots(stage) * count)
    return out


def attn_forward(r, p):
    lane = lax.broadcasted_iota(jnp.int32, (KP, 128), 1) < 64
    row = lax.broadcasted_iota(jnp.int32, (128, KP), 0) < 64
    zero = jnp.zeros((), BF16)
    g = p // 3
    bias = r.bias[g * 9 + p - g * 3]
    qkv = (nn(r.nin[...], r.wa[p, 0:D, :]) + bias).astype(BF16)
    r.qkv[p] = qkv
    kvc = nn(r.e[...], qkv[:, 128:]).astype(BF16)
    r.kvc[p] = kvc
    kc = kvc[:, :128] * jnp.asarray(0.125, BF16)
    kst = jnp.concatenate([jnp.where(lane, kc, zero), jnp.where(lane, zero, kc)], 0)
    r.s[...] = nt(kst, qkv[:, :128])
    for h in range(2):
        for t in range(4):
            rs, ts = pl.ds(h * KP, KP), pl.ds(t * 128, 128)
            s = r.s[rs, ts] + r.smask[:, ts]
            m = jnp.max(s, 0, keepdims=True)
            e = jnp.exp(s - m)
            inv = 1.0 / jnp.sum(e, 0, keepdims=True)
            r.p[p, rs, ts] = (e * inv).astype(BF16)
    vt = kvc[:, 128:].T
    lhs = jnp.concatenate([jnp.where(row, vt, zero), jnp.where(row, zero, vt)], 1)
    mt = nn(lhs, r.p[p]).astype(BF16)
    r.mixt[p] = mt
    r.mix[p] = mt.T


def w_out(r, p):
    return jnp.concatenate([r.wa[p, 768:896, :], r.wa[p, 896:1024, :]], 1)


def attn_backward(r, p, g, unit):
    lane = lax.broadcasted_iota(jnp.int32, (KP, 128), 1) < 64
    row = lax.broadcasted_iota(jnp.int32, (128, KP), 0) < 64
    zero = jnp.zeros((), BF16)
    dm = r.mix[p]
    kvc = r.kvc[p]
    qkv = r.qkv[p]
    vc = kvc[:, 128:]
    vst = jnp.concatenate([jnp.where(lane, vc, zero), jnp.where(lane, zero, vc)], 0)
    r.s[...] = nt(vst, dm)
    for h in range(2):
        for t in range(4):
            rs, ts = pl.ds(h * KP, KP), pl.ds(t * 128, 128)
            pr = r.p[p, rs, ts].astype(F32)
            dp = r.s[rs, ts]
            c = jnp.sum(pr * dp, 0, keepdims=True)
            r.ds[rs, ts] = (pr * (dp - c)).astype(BF16)
    dvs = nn(r.p[p], dm)
    dks = nn(r.ds[...], qkv[:, :128]) * 0.125
    dkv = jnp.concatenate([jnp.where(lane, dks[:KP], dks[KP:]), jnp.where(lane, dvs[:KP], dvs[KP:])], 1).astype(BF16)
    kt = (kvc[:, :128] * jnp.asarray(0.125, BF16)).T
    lhs = jnp.concatenate([jnp.where(row, kt, zero), jnp.where(row, zero, kt)], 1)
    dq = nn(lhs, r.ds[...]).astype(BF16).T
    dkvt = nn(r.et[...], dkv).astype(BF16)
    r.dcomp[...] += nt(dkv, qkv[:, 128:])
    dqkv = jnp.concatenate([dq, dkvt], 1)
    gw = nn(r.nint[...], dqkv).astype(BF16)
    for j in range(3):
        for ch in range(2):
            r.grad[unit, ch, g, j * 384:(j + 1) * 384, :] = gw[ch * 384:(ch + 1) * 384, j * 128:(j + 1) * 128]
    r.gbqkv[p] = jnp.sum(dqkv.astype(F32), 0, keepdims=True)
    r.dmid[...] += nt(dqkv, r.wa[p, 0:D, :])


def out_backward(r):
    for p in range(0, NP_, 2):
        dm = nt(r.drl[...], jnp.concatenate([w_out(r, p), w_out(r, p + 1)], 0)).astype(BF16)
        r.mix[p] = dm[:, :128]
        r.mix[p + 1] = dm[:, 128:]
    gw = nn(jnp.concatenate([r.mixt[p] for p in range(NP_)], 0), r.drl[...]).astype(BF16)
    for p in range(NP_):
        for j in range(6):
            lo = 1152 + (j % 3) * 128
            r.grad[6 + p % 3, j // 3, p // 3, lo:lo + 128, :] = gw[p * 128:(p + 1) * 128, j * 128:(j + 1) * 128]


def ffn_chunk(r, k, g):
    c = g * 6 + k
    wup = r.wf[c, 0:D, :]
    wdn = jnp.concatenate([r.wf[c, 768 + 256 * j:1024 + 256 * j, :] for j in range(3)], 1)
    bup = r.bias[g * 9 + 3 + k][:, :256]
    r.s[:, 0:256] = nn(r.nmid[...], wup)
    r.s[:, 256:512] = nt(r.cot[...], wdn)
    for i in range(8):
        rs = pl.ds(i * 64, 64)
        pre = r.s[rs, 0:256] + bup
        phi = 0.5 * (1.0 + lax.erf(pre * SQRT_HALF))
        pdf = jnp.exp(-0.5 * pre * pre) * INV_SQRT_TWO_PI
        r.ds[rs, 0:256] = (pre * phi).astype(BF16)
        r.ds[rs, 256:512] = (r.s[rs, 256:512] * (phi + pre * pdf)).astype(BF16)
    r.ffn[...] += nn(r.ds[:, 0:256], wdn)
    r.dmid[...] += nt(r.ds[:, 256:512], wup)
    gw = nn(r.ds[:, 0:256].T, r.cot[...]).astype(BF16)
    for j in range(6):
        lo = 768 + (j % 3) * 256
        r.grad[k, j // 3, g, lo:lo + 256, :] = gw[:, j * 128:(j + 1) * 128]
    gw = nn(r.nmidt[...], r.ds[:, 256:512]).astype(BF16)
    for ch in range(2):
        r.grad[k, ch, g, 0:768, :] = gw[:, ch * 128:(ch + 1) * 128]
    r.gbup[c] = jnp.sum(r.ds[:, 256:512].astype(F32), 0, keepdims=True)


def add_rows(dst, srcs, out=None):
    out = dst if out is None else out
    n = dst.shape[0]
    for lo in range(0, n, 384):
        rows = pl.ds(lo, min(384, n - lo))
        if len(srcs) == 1:
            out[rows, :] = dst[rows, :] + srcs[0][rows, :]
        else:
            out[rows, :] = functools.reduce(operator.add, [v[rows, :].astype(F32) for v in srcs], dst[rows, :].astype(F32)).astype(BF16)


def part_of(u):
    if isinstance(u, int):
        return u // SUB, pl.ds(u % SUB * PART, PART)
    return lax.div(u, SUB), pl.ds(pl.multiple_of(lax.rem(u, SUB) * PART, PART), PART)


class Reduce:
    def __init__(self, r, n):
        self.r = r
        b, h = lax.axis_index("batch"), lax.axis_index("head")
        self.b, self.h, self.c = b, h, lax.rem(b, 2)
        self.core = (b + 1 - 2 * self.c, h)
        self.flip = (b, 1 - h)
        self.orders = orders(n)
        self.families = len(self.orders)
        self.copies, self.places = copies(n), places(n)
        self.turn = lambda u: turn(u, n)

    def bit(self, stride):
        return lax.rem(lax.div(self.b, stride), 2)

    def across(self, stride):
        return (self.b + stride - 2 * stride * self.bit(stride), self.h)

    def peers(self, axis):
        if axis == HEAD:
            return self.h, [(1 - self.h, self.flip)]
        stride, size = axis
        a = lax.rem(lax.div(self.b, stride), size)
        if size == 2:
            return a, [(1 - a, self.across(stride))]
        ks = [lax.rem(a + j, size) for j in range(1, size)]
        return a, [(k, (self.b + (k - a) * stride, self.h)) for k in ks]

    def copy(self, src, dst, stage, u, dev, j=0):
        at = self.places[stage] + lax.rem(u, slots(stage)) * self.copies[stage] + j
        return lambda: pltpu.make_async_remote_copy(src_ref=src, dst_ref=dst, send_sem=self.r.rsend.at[at], recv_sem=self.r.rrecv.at[at],
                                                    device_id=dev, device_id_type=MESH)

    def exchanges(self, u, family, bufs):
        grad, rc, halves, fin = bufs
        one = rc.shape[0] == 1
        h, c, order = self.h, self.c, self.orders[family]
        slot = 0 if one else lax.rem(u, slots(0))
        none = lambda: None

        def core_add():
            for g in range(2):
                add_rows(grad.at[c, g], [rc.at[slot, g]])
        stages = [([self.copy(grad.at[1 - c], rc.at[slot], 0, u, self.core)], core_add)]
        base, part, both, gathers = 0, grad.shape[2], True, []
        for i, axis in enumerate(order):
            buf, last = halves[i], i == len(order) - 1
            place, others = self.peers(axis)
            if axis == HEAD or part % (8 * axis[1]):
                rows = pl.ds(base, part)
                sends = [(rows, dev) for _, dev in others]
            else:
                part //= axis[1]
                sends = [(pl.ds(pl.multiple_of(base + k * part, part), part), dev) for k, dev in others]
                base = pl.multiple_of(base + place * part, part)
                rows = pl.ds(base, part)
                gathers.append((axis, base, part))
            if axis == HEAD:
                both = False
                moves = [(1 - h, h)]
            else:
                moves = [(0, 0), (1, 1)] if both else [(h, h)]
            cps, adds = [], []
            for give, keep in moves:
                lands = []
                for send, dev in sends:
                    land = buf.at[0 if one else lax.rem(u, slots(1 + i)), pl.ds(len(cps) * part, part)]
                    cps.append(self.copy(grad.at[c, give, send], land, 1 + i, u, dev, len(cps)))
                    lands.append(land)
                adds.append((keep, lands))

            def add(adds=adds, rows=rows, last=last):
                for g, lands in adds:
                    add_rows(grad.at[c, g, rows], lands, fin.at[c, rows] if last else None)
            stages.append((cps, add))
        for axis, lo, count in reversed(gathers):
            own = fin.at[c, pl.ds(lo, count)]
            stages.append(([self.copy(own, own, len(stages), u, dev, j) for j, (_, dev) in enumerate(self.peers(axis)[1])], none))
        stages.append(([self.copy(fin.at[c], fin.at[c], len(stages), u, self.core)], none))
        return stages

    def lags(self):
        count = len(self.exchanges(0, 0, self.bufs(0)))
        out = [0]
        for i in range(count):
            out.append(out[-1] + gap(i))
        return out

    def small(self):
        r = self.r
        return (r.cgrad, r.crc, r.chalves, r.out_comp)

    def bufs(self, u):
        r = self.r
        at, rows = part_of(u)
        return (r.grad.at[at, :, :, rows], r.rc, r.halves, r.out_grad.at[at, :, rows])

    def step(self, u, i, family, bufs):
        st = self.exchanges(u, family, bufs)
        if i > len(st):
            return
        if i > 0:
            for cp in st[i - 1][0]:
                cp().wait()
            st[i - 1][1]()
        if i < len(st):
            for cp in st[i][0]:
                cp().start()

    def tick(self, i, lags, static):
        for s in reversed(range(len(lags))):
            u = i - lags[s]
            if static:
                if 0 <= u < TOTAL:
                    self.step(u, s, self.turn(u), self.bufs(u))
                elif u == TOTAL:
                    self.step(u, s, 0, self.small())
                continue
            if s == 0:
                @pl.when((u >= 0) & (u < TOTAL))
                def _(s=s, u=u):
                    self.step(u, s, 0, self.bufs(u))
                continue
            for f in range(self.families):
                even = lax.rem(u, 2) == 0
                here = u >= 0
                if self.families > 1:
                    here = ((u < 12) | jnp.logical_not(even), even & (u >= 12) & (u < 24), even & (u >= 24))[f]

                @pl.when((u >= 0) & (u < TOTAL) & here)
                def _(s=s, u=u, f=f):
                    self.step(u, s, f, self.bufs(u))


class Gather:
    def __init__(self, r, red):
        self.r = r
        self.h = red.h
        c, x, z = red.bit(1), red.bit(2), red.bit(4)
        self.q = (c * 4 + z * 2 + x, c * 4 + x * 2 + z)
        self.dev = [(red.flip, red.across(2), red.across(4), red.core), (red.flip, red.across(4), red.across(2), red.core)]

    def copy(self, u, stage, attn, odd):
        h = self.h
        g = h if stage == 0 else 1 - h
        unit = self.r.wa.at[g * 3 + u] if attn else self.r.wf.at[g * 6 + u - 3]
        piece = unit.shape[0] // 8
        count = 1 if stage == 0 else 1 << (stage - 1)
        lo = lax.div(self.q[odd], count) * count * piece
        view = unit.at[pl.ds(pl.multiple_of(lo, piece), count * piece)]
        return pltpu.make_async_remote_copy(src_ref=view, dst_ref=view, send_sem=self.r.gsend.at[u, stage], recv_sem=self.r.grecv.at[u, stage],
                                            device_id=self.dev[odd][stage], device_id_type=MESH)

    def start(self, u):
        self.copy(u, 0, u < 3, u % 2).start()

    def step(self, u, stage):
        self.copy(u, stage - 1, u < 3, u % 2).wait()
        if stage < 4:
            self.copy(u, stage, u < 3, u % 2).start()

    def ready(self, u, attn):
        for odd in range(2):
            @pl.when(lax.rem(u, 2) == odd)
            def _(odd=odd):
                self.copy(u, 3, attn, odd).wait()


def layer(n, names, refs):
    r = Refs()
    for name, ref in zip(names, refs):
        setattr(r, name, ref)
    steps = len(orders(n)[0])
    r.halves = [getattr(r, "half%d" % i) for i in range(steps)]
    r.chalves = [getattr(r, "chalf%d" % i) for i in range(steps)]
    red = Reduce(r, n)
    gat = Gather(r, red)
    b, h = red.b, red.h

    barrier = pltpu.get_barrier_semaphore()
    peers = [red.core] + [dev for axis in red.orders[0] for _, dev in red.peers(axis)[1]]
    for dev in peers:
        pl.semaphore_signal(barrier, inc=1, device_id=dev, device_id_type=MESH)

    hs = pl.ds(pl.multiple_of(h * 256, 256), 256)
    cs = pl.ds(pl.multiple_of(h * 128, 128), 128)
    homes = [r.wa.at[h * 3 + u] for u in range(3)] + [r.wf.at[h * 6 + k] for k in range(6)] + [r.x.at[hs], r.comp.at[cs], r.cot.at[hs]]

    def load(key, src, dst):
        pltpu.make_async_copy(src, dst, r.lsem.at[key]).start()

    def loaded(key):
        pltpu.make_async_copy(homes[key], homes[key], r.lsem.at[key]).wait()

    def swap(i, src, dst):
        return pltpu.make_async_remote_copy(src_ref=src, dst_ref=dst, send_sem=r.ssend.at[i], recv_sem=r.srecv.at[i],
                                            device_id=red.flip, device_id_type=MESH)
    quarter = pl.ds(pl.multiple_of(h * 128 + red.c * 64, 64), 64)
    far_quarter = pl.ds(pl.multiple_of((1 - h) * 128 + red.c * 64, 64), 64)
    share = pltpu.make_async_remote_copy(src_ref=r.comp.at[far_quarter], dst_ref=r.comp.at[far_quarter], send_sem=r.ssend.at[6], recv_sem=r.srecv.at[6],
                                         device_id=red.core, device_id_type=MESH)
    bs = r.bias.at[pl.ds(h * 9, 9)]
    swaps = [swap(0, r.inputs.at[1 - h], r.x.at[hs]), swap(1, r.compress.at[pl.ds(pl.multiple_of(red.c * 64, 64), 64)], r.comp.at[quarter]), swap(2, bs, bs),
             swap(3, r.cotangent.at[1 - h], r.cot.at[hs])]
    for u in range(3):
        unit, cols = r.wa.at[h * 3 + u], pl.ds(u * 128, 128)
        for j, w in enumerate((r.w_query, r.w_key, r.w_value)):
            load(u, w.at[:, cols], unit.at[0:768, j * 128:(j + 1) * 128])
        for j in range(2):
            load(u, r.w_out.at[cols, j * 384:(j + 1) * 384], unit.at[768 + 128 * j:896 + 128 * j])
    pl.semaphore_wait(barrier, len(peers))
    for u in range(3):
        loaded(u)
        gat.start(u)
    swaps[1].start()
    swaps[0].start()
    load(9, r.inputs.at[h], r.x.at[hs])
    load(10, r.compress, r.comp.at[cs])
    for k in range(6):
        unit = r.wf.at[h * 6 + k]
        load(3 + k, r.w_up.at[:, k * 256:(k + 1) * 256], unit.at[0:768])
        for j in range(3):
            load(3 + k, r.w_down.at[k * 256:(k + 1) * 256, j * 256:(j + 1) * 256], unit.at[768 + 256 * j:1024 + 256 * j])
    load(11, r.cotangent.at[h], r.cot.at[hs])
    bqkv = [row_vec(v) for v in (r.b_query, r.b_key, r.b_value)]
    bup = row_vec(r.b_up)
    for u in range(3):
        r.bias[h * 9 + u] = jnp.concatenate([v[:, u * 128:(u + 1) * 128] for v in bqkv], 1)
    for k in range(6):
        r.bias[h * 9 + 3 + k, :, 0:256] = bup[:, k * 256:(k + 1) * 256]
        r.bias[h * 9 + 3 + k, :, 256:384] = jnp.zeros((1, 128), F32)
    swaps[2].start()
    for u in range(3, 9):
        loaded(u)
        gat.start(u)
        if u == 4:
            swaps[3].start()

    seg = r.seg_ids[pl.ds(h, 1), :]
    pad = r.pad_mask[pl.ds(h, 1), :]
    jj = lax.broadcasted_iota(jnp.int32, (KP, T), 0)
    tt = lax.broadcasted_iota(jnp.int32, (KP, T), 1)
    slot = jnp.sum(jnp.where(tt == 2 * jj, seg, 0), 1, keepdims=True)
    same = slot == seg
    r.smask[...] = jnp.where(same, 0.0, -1e30)
    r.keep[...] = jnp.where(same & (pad == 0), 1.0, 0.0).astype(BF16)
    gain_a, shift_a, b_out, gain_f, shift_f, b_down = (row_vec(v) for v in (r.attn_gain, r.attn_shift, r.b_out, r.ffn_gain, r.ffn_shift, r.b_down))
    for u, stage in ((0, 1), (1, 1), (0, 2), (2, 1), (1, 2)):
        gat.step(u, stage)
    swaps[1].wait()
    share.start()
    gat.step(0, 3)
    gat.step(2, 2)

    def ln1(rs):
        xh, _ = norm_stats(r.x[rs, :].astype(F32))
        r.nin[rs, :] = (xh * gain_a + shift_a).astype(BF16)

    def ln1_half(g):
        blocks(256, 64, lambda rs: ln1(pl.ds(pl.multiple_of(g * 256 + rs.start, 64), 64)))
    loaded(9)
    ln1_half(h)
    swaps[0].wait()
    gat.step(1, 3)
    ln1_half(1 - h)
    r.nint[...] = r.nin[...].T
    loaded(10)
    share.wait()
    swaps[2].wait()
    e = jnp.where(r.keep[...].astype(F32) > 0.5, r.comp[...].astype(F32), 0.0)
    r.e[...] = e.astype(BF16)
    r.et[...] = e.T.astype(BF16)

    def hook(i, table):
        for at, todo in sorted(table.items()):
            @pl.when(i == at)
            def _(todo=todo):
                for u, stage in todo:
                    gat.step(u, stage)
    fore = {0: [(2, 3)], 1: [(3, 1)], 3: [(4, 1)], 4: [(3, 2)], 5: [(4, 2)]}

    def pair(i, carry):
        far = lax.div(i, 3)
        g = lax.rem(h + far, 2)
        pp = i - 3 * far

        @pl.when(far == 1)
        def _():
            gat.ready(pp, True)
        attn_forward(r, g * 3 + pp)
        hook(i, fore)
        return carry
    lax.fori_loop(0, 6, pair, 0)

    r.res[...] = nn(jnp.concatenate([r.mix[p] for p in range(NP_)], 1), jnp.concatenate([w_out(r, p) for p in range(NP_)], 0))

    def proj(rs):
        res = r.x[rs, :].astype(F32) + (r.res[rs, :] + b_out)
        r.res[rs, :] = res
        xh, _ = norm_stats(res)
        r.nmid[rs, :] = (xh * gain_f + shift_f).astype(BF16)
        r.ffn[rs, :] = res + b_down
        r.dmid[rs, :] = jnp.zeros_like(res)
    blocks(T, 64, proj)
    r.nmidt[...] = r.nmid[...].T
    loaded(11)
    swaps[3].wait()

    lags = red.lags()

    def ticks(group):
        for j in range(SUB // 2):
            red.tick(group * (SUB // 2) + j, lags, False)

    late = {0: [(3, 3)], 1: [(4, 3)], 2: [(5, 1), (6, 1)], 3: [(5, 2), (7, 1)], 4: [(6, 2), (8, 1)], 5: [(7, 2), (5, 3)], 6: [(8, 2)], 7: [(6, 3)],
            8: [(7, 3)], 9: [(8, 3)]}

    def main(i, carry):
        far = (1 - lax.rem(i, 2)) * jnp.minimum(i, 1) + lax.div(i, 11)
        k = lax.div(i + 1 - 2 * far, 2)

        @pl.when(far == 1)
        def _():
            gat.ready(3 + k, False)
        ffn_chunk(r, k, lax.rem(h + far, 2))
        hook(i, late)

        @pl.when(i > 1)
        def _():
            ticks(i - 2)
        return carry
    lax.fori_loop(0, 12, main, 0)

    r.vec[0] = jnp.zeros((16, D), F32)

    def ln2b(rs):
        xh, rstd = norm_stats(r.res[rs, :])
        dm = r.dmid[rs, :]
        cot = r.cot[rs, :].astype(F32)
        d = cot + norm_back(dm, xh, rstd, gain_f)
        r.res[rs, :] = d
        r.drl[rs, :] = d.astype(BF16)
        r.nmid[rs, :] = r.ffn[rs, :].astype(BF16)
        for i, v in ((2, d), (3, dm * xh), (4, dm), (5, cot)):
            r.vec[0, i:i + 1, :] += jnp.sum(v, 0, keepdims=True)
        r.dmid[rs, :] = jnp.zeros_like(d)
    blocks(T, 64, ln2b)
    ticks(10)
    r.dcomp[...] = jnp.zeros_like(r.dcomp)
    out_backward(r)

    def back(i, carry):
        pp = lax.div(i, 2)
        g = lax.rem(h + i, 2)
        attn_backward(r, g * 3 + pp, g, 6 + pp)
        ticks(11 + i)
        return carry
    lax.fori_loop(0, 6, back, 0)
    gc = jnp.where(r.keep[...].astype(F32) > 0.5, r.dcomp[...], 0.0).astype(BF16)
    for g in range(2):
        for j in range(4):
            lo = (j % 2) * 128
            r.cgrad[j // 2, g, lo:lo + 128, :] = gc[g * 128:(g + 1) * 128, j * 128:(j + 1) * 128]

    def ln1b(rs):
        xh, rstd = norm_stats(r.x[rs, :].astype(F32))
        dn = r.dmid[rs, :]
        r.nin[rs, :] = (r.res[rs, :] + norm_back(dn, xh, rstd, gain_a)).astype(BF16)
        r.vec[0, 0:1, :] += jnp.sum(dn * xh, 0, keepdims=True)
        r.vec[0, 1:2, :] += jnp.sum(dn, 0, keepdims=True)
    blocks(T, 64, ln1b)
    for g in range(2):
        for i in range(2):
            at = 6 + g * 2 + i
            r.vec[0, at:at + 1, :] = jnp.concatenate([r.gbup[g * 6 + 3 * i + j] for j in range(3)], 1)
    for j in range(3):
        r.vec[0, 10 + j:11 + j, :] = jnp.concatenate([r.gbqkv[p][:, j * 128:(j + 1) * 128] for p in range(NP_)], 1)

    bits = [red.flip]
    s = 1
    while s < n:
        v = lax.rem(lax.div(b, s), 2)
        bits.append((b + s - 2 * s * v, h))
        s *= 2

    def vec_copy(i):
        return pltpu.make_async_remote_copy(src_ref=r.vec.at[i], dst_ref=r.vrecv.at[i], send_sem=r.vsend.at[i], recv_sem=r.vrsem.at[i],
                                            device_id=bits[i], device_id_type=MESH)

    def vec_step(i):
        if i > 0:
            vec_copy(i - 1).wait()
            r.vec[i] = r.vec[i - 1] + r.vrecv[i - 1]
        if i < len(bits):
            vec_copy(i).start()

    hs_far = pl.ds(pl.multiple_of((1 - h) * 256, 256), 256)
    backs = []
    for i, (src, dst) in enumerate(((r.nmid, r.out_y), (r.nin, r.out_ig))):
        backs.append(swap(4 + i, src.at[hs_far], dst.at[h]))
        dst[h] = src[hs, :]
    vec_step(0)
    first = 17 * (SUB // 2)
    stride = max(1, (TOTAL + lags[-1] - first) // (len(bits) + 1))
    for i in range(first, TOTAL + lags[-1] + 1):
        red.tick(i, lags, True)
        if i > first and (i - first) % stride == 0 and (i - first) // stride <= len(bits):
            vec_step((i - first) // stride)
        if i == TOTAL - 1 + lags[2]:
            for cp in backs:
                cp.start()
    r.out_vec[...] = r.vec[len(bits)]
    for cp in backs:
        cp.wait()


ARGS = ["inputs", "cotangent", "seg_ids", "pad_mask", "attn_gain", "attn_shift", "w_query", "w_key", "w_value", "b_query", "b_key", "b_value",
        "compress", "w_out", "b_out", "ffn_gain", "ffn_shift", "w_up", "b_up", "w_down", "b_down"]
IN_HBM = ["inputs", "cotangent", "w_query", "w_key", "w_value", "compress", "w_out", "w_up", "w_down"]


def run_layer(n, args):
    bits = n.bit_length()
    out = dict(out_y=((2, 256, D), BF16), out_ig=((2, 256, D), BF16), out_grad=((UNITS, 2, ROWS, 128), BF16), out_comp=((2, 256, 128), BF16), out_vec=((16, D), F32))
    scr = dict(x=((T, D), BF16), cot=((T, D), BF16), comp=((KP, T), BF16), bias=((18, 1, 384), F32), wa=((NP_, 1024, 384), BF16), wf=((NF, ROWS, 256), BF16),
               e=((KP, T), BF16), et=((T, KP), BF16), smask=((KP, T), F32), keep=((KP, T), BF16), nin=((T, D), BF16), nint=((D, T), BF16),
               qkv=((NP_, T, 384), BF16), kvc=((NP_, KP, 256), BF16), s=((512, T), F32), p=((NP_, 512, T), BF16), ds=((512, T), BF16),
               mixt=((NP_, 128, T), BF16), mix=((NP_, T, 128), BF16), res=((T, D), F32), nmid=((T, D), BF16), nmidt=((D, T), BF16),
               ffn=((T, D), F32), dmid=((T, D), F32), drl=((T, D), BF16), dcomp=((KP, T), F32),
               vec=((bits + 1, 16, D), F32), vrecv=((bits, 16, D), F32),
               gbup=((NF, 1, 256), F32), gbqkv=((NP_, 1, 384), F32), grad=((UNITS, 2, 2, ROWS, 128), BF16), cgrad=((2, 2, 256, 128), BF16))
    steps = len(orders(n)[0])
    for pre, rows in (("", PART), ("c", 256)):
        scr[pre + "rc"] = ((slots(0) if pre == "" else 1, 2, rows, 128), BF16)
        for i in range(steps):
            scr["%shalf%d" % (pre, i)] = ((slots(1 + i) if pre == "" else 1, max(landing(rows, order)[i] for order in orders(n)), 128), BF16)
    sems = dict(rsend=(places(n)[-1],), rrecv=(places(n)[-1],), gsend=(9, 4), grecv=(9, 4), ssend=(7,), srecv=(7,), vsend=(bits,), vrsem=(bits,),
                lsem=(12,))
    names = ARGS + list(out) + list(scr) + list(sems)
    hbm, vmem = pl.BlockSpec(memory_space=pl.ANY), pl.BlockSpec(memory_space=pltpu.VMEM)
    return pl.pallas_call(
        lambda *refs: layer(n, names, refs),
        out_shape=[pltpu.VMEM(*v) for v in out.values()],
        in_specs=[hbm if a in IN_HBM else vmem for a in ARGS], out_specs=[vmem] * len(out),
        scratch_shapes=[pltpu.VMEM(*v) for v in scr.values()] + [pltpu.SemaphoreType.DMA(v) for v in sems.values()],
        compiler_params=pltpu.CompilerParams(collective_id=0, has_side_effects=True, vmem_limit_bytes=55 * MIB), name="layer")(*args)


def finish(refs):
    (y_in, ig_in, g_in, c_in, v_in, y, ig, gain_a, shift_a, wq, wk, wv, bq, bk, bv, comp, wo, bo, gain_f, shift_f, wu, bu, wd, bd,
     fa, fo, fu, fd, fc, osem) = refs
    h = lax.axis_index("head")
    outs = iter(range(64))
    pend = []

    def put(src, dst):
        cp = pltpu.make_async_copy(src, dst, osem.at[next(outs)])
        cp.start()
        pend.append(cp)
    put(y_in, y)
    put(ig_in, ig)
    for i, o in enumerate((gain_a, shift_a, bo, gain_f, shift_f, bd)):
        o[...] = v_in[i, :]
    for i, o in enumerate((bq, bk, bv)):
        v = v_in[10 + i:11 + i, :]
        o[...] = jnp.where(h == 0, v[:, :384], v[:, 384:]).reshape(384)
    v = jnp.where(h == 0, v_in[6:8, :], v_in[8:10, :])
    bu[...] = jnp.concatenate([v[0:1], v[1:2]], 1).reshape(1536)
    for k in range(6):
        for ch in range(2):
            fu[k, :, ch * 128:(ch + 1) * 128] = g_in[k, ch, 0:768, :].astype(F32)
            for j in range(3):
                at = (ch * 3 + j) * 128
                fd[k, :, at:at + 128] = g_in[k, ch, 768 + j * 256:1024 + j * 256, :].astype(F32)
        put(fu.at[k], wu.at[:, k * 256:(k + 1) * 256])
        put(fd.at[k], wd.at[k * 256:(k + 1) * 256])
    for p in range(3):
        u = 6 + p
        for ch in range(2):
            for j in range(3):
                fa[j, ch * 384:(ch + 1) * 384, p * 128:(p + 1) * 128] = g_in[u, ch, j * 384:(j + 1) * 384, :].astype(F32)
                at = (ch * 3 + j) * 128
                fo[p, :, at:at + 128] = g_in[u, ch, 1152 + j * 128:1280 + j * 128, :].astype(F32)
        put(fo.at[p], wo.at[p * 128:(p + 1) * 128])
    for j, o in enumerate((wq, wk, wv)):
        put(fa.at[j], o)
    for j in range(4):
        fc[:, j * 128:(j + 1) * 128] = c_in[j // 2, (j % 2) * 128:(j % 2) * 128 + 128, :].astype(F32)
    put(fc, comp)
    for cp in pend:
        cp.wait()


def run_finish(parts):
    hbm, vmem = pl.BlockSpec(memory_space=pl.ANY), pl.BlockSpec(memory_space=pltpu.VMEM)
    f = lambda *s: jax.ShapeDtypeStruct(s, F32)
    row = jax.ShapeDtypeStruct((2, 256, D), BF16)
    outs = [(row, hbm), (row, hbm), (f(D), vmem), (f(D), vmem), (f(D, 384), hbm), (f(D, 384), hbm), (f(D, 384), hbm), (f(384), vmem), (f(384), vmem), (f(384), vmem),
            (f(128, T), hbm), (f(384, D), hbm), (f(D), vmem), (f(D), vmem), (f(D), vmem), (f(D, 1536), hbm), (f(1536), vmem), (f(1536, D), hbm), (f(D), vmem)]
    scr = [((3, D, 384), F32), ((3, 128, D), F32), ((6, D, 256), F32), ((6, 256, D), F32), ((128, T), F32)]
    return pl.pallas_call(
        lambda *refs: finish(refs), out_shape=[o for o, _ in outs], in_specs=[vmem] * 5, out_specs=[s for _, s in outs],
        scratch_shapes=[pltpu.VMEM(*v) for v in scr] + [pltpu.SemaphoreType.DMA((64,))],
        compiler_params=pltpu.CompilerParams(vmem_limit_bytes=40 * MIB), name="finish")(*parts)


def solution(mesh):
    n = mesh.shape["batch"]

    def on_device(*args):
        return tuple(run_finish(run_layer(n, args)))

    tok, rep, col, vec, row = P("batch", "head", None), P(), P(None, "head"), P("head"), P("head", None)
    ids = P("batch", None)
    return jax.shard_map(
        on_device, mesh=mesh,
        in_specs=(tok, tok, ids, ids, rep, rep, col, col, col, vec, vec, vec, row, row, rep, rep, rep, col, vec, row, rep),
        out_specs=(tok, tok, rep, rep, col, col, col, vec, vec, vec, row, row, rep, rep, rep, col, vec, row, rep),
        check_vma=False)
```
